128 devices in a mesh: sweep: 8 (over y, core), leaf: 16 (over x, z).
Axes of the slice: x: 4, y: 4, z: 4, core: 2. Of those that a mesh axis runs over, the one named last changes fastest.
Arguments:
- rhs_interior: float32 [8, 16, 2, 4, 1024], P('sweep', 'leaf'), may hold values from -6 to 6
- rhs_separator: float32 [8, 2, 4, 2560], P('sweep', None, None, 'leaf'), may hold values from -6 to 6
- leaf_inverse: bfloat16 [8, 16, 2, 1024, 1024], P('sweep', 'leaf'), may hold values from -1.2 to 1.2
- leaf_to_front: bfloat16 [8, 16, 2, 256, 2560], P('sweep', 'leaf'), may hold values from -0.09375 to 0.09375
- front_to_leaf: bfloat16 [8, 16, 2, 2560, 256], P('sweep', 'leaf'), may hold values from -0.0390625 to 0.0390625
- front_inverse: bfloat16 [8, 2, 2560, 2560], P('sweep', None, None, 'leaf'), may hold values from -1.2 to 1.2
- front_sizes: int32 [8, 16], P('sweep', 'leaf'), may hold values from 1 to 768, 9216 in all within a row
Outputs:
- sol_interior: float32 [8, 16, 2, 4, 1024], P('sweep', 'leaf')
- sol_separator: float32 [8, 2, 4, 2560], P('sweep', None, None, 'leaf')
The draws below stay inside these ranges and needn't reach their ends.
Inputs may be any that keep to these rules, and one draw needn't show every extreme that they name: `front_sizes`: in each panel the values sum to 9216 and one of them equals 768.
All inputs are finite; a program needn't handle non-finite values. No bound on the sum of `front_sizes` on one device may be relied on, other than what follows from the above.
Results may differ from the reference program's by a relative error of at most 0.038.
Values may be sent and summed in bfloat16 or wider, within the bound.
A program may use at most 128 MiB of HBM per device.

```python
import math
import jax
import jax.numpy as jnp
import numpy as np
from jax import lax

LEAF_CELLS = 1024
PORT_CELLS = 256
SEPARATOR = 2560
PLANES = 4
SOURCES = 4
PANELS = 8
LEAVES = 16


def structured_inverse(key, leading, extent):
    spread = 0.4 / math.sqrt(2.0 * extent)
    key_random, key_far, key_near, key_far_phase, key_near_phase = jax.random.split(key, 5)
    full_shape = leading + (2, extent, extent)
    cell_shape = leading + (extent,)
    random_part = jax.random.truncated_normal(key_random, -4.0, 4.0, full_shape, jnp.float32)
    far_gain = jax.random.uniform(key_far, cell_shape, jnp.float32, 0.8, 0.95)
    near_gain = jax.random.uniform(key_near, cell_shape, jnp.float32, 0.4, 0.6)
    far_phase = jax.random.uniform(key_far_phase, cell_shape, jnp.float32, -math.pi, math.pi)
    near_phase = jax.random.uniform(key_near_phase, cell_shape, jnp.float32, -math.pi, math.pi)
    far_pair = jnp.stack([far_gain * jnp.cos(far_phase), far_gain * jnp.sin(far_phase)], axis=-2)[..., None]
    near_pair = jnp.stack([near_gain * jnp.cos(near_phase), near_gain * jnp.sin(near_phase)], axis=-2)[..., None]
    in_index = lax.broadcasted_iota(jnp.int32, (extent, extent), 0)
    out_index = lax.broadcasted_iota(jnp.int32, (extent, extent), 1)
    same_cell = in_index // PLANES == out_index // PLANES
    mirror_mask = same_cell & (in_index % PLANES + out_index % PLANES == PLANES - 1)
    same_mask = in_index == out_index
    result = spread * random_part
    result = result + jnp.where(mirror_mask, far_pair, jnp.float32(0.0))
    result = result + jnp.where(same_mask, near_pair, jnp.float32(0.0))
    return result.astype(jnp.bfloat16)


def draw_leaf_inverse(key, part):
    return structured_inverse(jax.random.fold_in(key, 11), (PANELS, LEAVES), LEAF_CELLS)


def draw_front_inverse(key, part):
    return structured_inverse(jax.random.fold_in(key, 23), (PANELS,), SEPARATOR)


def strengthened(array, rng, source, target, parts, factor):
    owner, partner = [(jnp.arange(array.shape[dim]) // (array.shape[dim] // parts)).reshape([-1 if axis == dim else 1 for axis in range(array.ndim)]) for dim in (source, target)]
    chosen = jax.random.permutation(rng, parts)[partner]
    strong = (owner == chosen) | (owner == (partner + parts // 2) % parts)
    return jnp.where(strong, factor * array, array)


def shard_levels(key, shape, cuts, low, high):
    def one(axis_at, blocks):
        draws = jax.random.uniform(jax.random.fold_in(jax.random.fold_in(key, 6), axis_at), (blocks,), jnp.float32, low / len(cuts), high / len(cuts))
        return jnp.repeat(jnp.exp(draws), shape[axis_at] // blocks).reshape((-1,) + (1,) * (len(shape) - axis_at - 1))

    loudness = one(*cuts[0])
    for cut in cuts[1:]:
        loudness = loudness * one(*cut)
    return loudness


def split_up(count, total, most, slope):
    loads = [(1 << 20) // math.isqrt(standing ** slope) + 1 for standing in range(2, count + 1)]
    surplus, counts = total - most - (count - 1), [1] * (count - 1)
    while surplus > 0:
        movable = [i for i in range(count - 1) if counts[i] < most]
        mass, left = sum([loads[i] for i in movable]), surplus
        for i in movable:
            extra = min(most - counts[i], max(1, left * loads[i] // mass), surplus)
            counts[i] = counts[i] + extra
            surplus = surplus - extra
    return np.array([most] + counts)


def uneven_parts(rng, number_of, total, most, slope):
    if number_of == 2:
        one = jax.random.randint(rng, (), max(1, total - most), min(most, total - 1) + 1)
        return jnp.stack([one, total - one])
    tallies = jnp.asarray(split_up(number_of, total, most, slope), jnp.int32)
    couples = (number_of - 1) // 2
    giver, taker = tallies[1:1 + 2 * couples:2], tallies[2:2 + 2 * couples:2]
    room = jnp.minimum(giver - 1, most - taker)
    passed = jax.random.randint(jax.random.fold_in(rng, 1), (couples,), 0, 1 << 20) % (room + 1)
    tallies = tallies.at[1:1 + 2 * couples:2].set(giver - passed).at[2:2 + 2 * couples:2].set(taker + passed)
    return tallies[jax.random.permutation(jax.random.fold_in(rng, 2), number_of)]


def normal_values(own_key, dims, width, reach, pieces=(), kind=jnp.bfloat16):
    drawn = jax.random.normal(own_key, dims, jnp.float32) * width
    if len(pieces) > 0:
        drawn = shard_levels(own_key, dims, pieces, -0.22, 0.18) * drawn
    return jnp.clip(drawn, min=-reach, max=reach).astype(kind)


def heavy_noise(key, dims, width, limit, shards, heavy, held_as=jnp.bfloat16):
    array = width * jax.random.normal(key, dims, jnp.float32)
    if shards:
        array = array * shard_levels(key, dims, shards, -0.22, 0.18)
    return jnp.clip(strengthened(array, jax.random.fold_in(key, 3), *heavy), -limit, limit).astype(held_as)


def setup_inputs(seed: int = 0) -> dict:
    splits = jax.random.split(jax.random.key(seed), 8)
    return {
        "rhs_interior": normal_values(splits[0], (PANELS, LEAVES, 2, SOURCES, LEAF_CELLS), 1.0, 6.0, ((0, 8), (1, 16)), jnp.float32),
        "rhs_separator": normal_values(splits[1], (PANELS, 2, SOURCES, SEPARATOR), 1.0, 6.0, ((0, 8), (3, 16)), jnp.float32),
        "leaf_inverse": draw_leaf_inverse(jax.random.fold_in(splits[7], 71), 0),
        "leaf_to_front": heavy_noise(splits[3], (PANELS, LEAVES, 2, PORT_CELLS, SEPARATOR), (2 * PORT_CELLS * LEAVES) ** -0.5, 0.09375, ((0, 8), (1, 16)), (1, 4, 16, 2.0)),
        "front_to_leaf": normal_values(splits[4], (PANELS, LEAVES, 2, SEPARATOR, PORT_CELLS), (8 * SEPARATOR) ** -0.5, 0.0390625, ((0, 8), (1, 16))),
        "front_inverse": draw_front_inverse(jax.random.fold_in(splits[7], 71), 0),
        "front_sizes": jax.vmap(lambda own: uneven_parts(own, LEAVES, 3 * (LEAF_CELLS - PORT_CELLS) * LEAVES // 4, LEAF_CELLS - PORT_CELLS, 2))(jax.random.split(splits[6], PANELS)).reshape((PANELS, LEAVES)).astype(jnp.int32),
    }


coupling = 1.0


def cmul(vec, mat):
    rows = vec.reshape(-1, vec.shape[-1])
    part_re = jnp.dot(rows, mat[0], preferred_element_type=jnp.float32).reshape(2, -1, mat.shape[2])
    part_im = jnp.dot(rows, mat[1], preferred_element_type=jnp.float32).reshape(2, -1, mat.shape[2])
    return jnp.stack([part_re[0] - part_im[1], part_im[0] + part_re[1]])


def plane_of(values, plane):
    shaped = values.reshape(values.shape[:-1] + (values.shape[-1] // PLANES, PLANES))
    return shaped[..., plane]


def put_plane(values, plane):
    spread = jnp.repeat(values, PLANES, axis=-1)
    position = lax.broadcasted_iota(jnp.int32, spread.shape, spread.ndim - 1) % PLANES
    return jnp.where(position == plane, spread, jnp.zeros_like(spread))


def panel_solve(h_int, h_sep, inv_leaf, to_front, to_leaf, inv_front, live_mask):
    h_int = h_int * live_mask[:, None, None, :]

    def leaf_first(items):
        rhs_leaf, inverse, coupling_up = items
        inner = cmul(rhs_leaf.astype(jnp.bfloat16), inverse)
        leaf_term = cmul(inner[..., :PORT_CELLS].astype(jnp.bfloat16), coupling_up)
        return inner, leaf_term

    inner, terms = lax.map(leaf_first, (h_int, inv_leaf, to_front))
    front_rhs = h_sep - jnp.sum(terms, axis=0)
    front_sol = cmul(front_rhs.astype(jnp.bfloat16), inv_front)
    front_low = front_sol.astype(jnp.bfloat16)

    def leaf_second(items):
        inner_leaf, inverse, coupling_down = items
        port_corr = cmul(front_low, coupling_down)
        return inner_leaf - cmul(port_corr.astype(jnp.bfloat16), inverse[:, :PORT_CELLS, :])

    leaf_sol = lax.map(leaf_second, (inner, inv_leaf, to_leaf)) * live_mask[:, None, None, :]
    return leaf_sol, front_sol


def reference(rhs_interior, rhs_separator, leaf_inverse, leaf_to_front, front_to_leaf, front_inverse, front_sizes):
    positions = jnp.arange(LEAF_CELLS, dtype=jnp.int32)
    live_all = (positions[None, None, :] < PORT_CELLS + front_sizes[:, :, None]).astype(jnp.float32)
    fwd_int = []
    fwd_sep = []
    prev_int = jnp.zeros(rhs_interior.shape[1:], jnp.float32)
    prev_sep = jnp.zeros(rhs_separator.shape[1:], jnp.float32)
    for panel in range(PANELS):
        h_int = rhs_interior[panel] + coupling * put_plane(plane_of(prev_int, PLANES - 1), 0)
        h_sep = rhs_separator[panel] + coupling * put_plane(plane_of(prev_sep, PLANES - 1), 0)
        prev_int, prev_sep = panel_solve(h_int, h_sep, leaf_inverse[panel], leaf_to_front[panel], front_to_leaf[panel], front_inverse[panel], live_all[panel])
        fwd_int.append(prev_int)
        fwd_sep.append(prev_sep)
    sol_int = list(fwd_int)
    sol_sep = list(fwd_sep)
    for panel in reversed(range(PANELS - 1)):
        h_int = coupling * put_plane(plane_of(sol_int[panel + 1], 0), PLANES - 1)
        h_sep = coupling * put_plane(plane_of(sol_sep[panel + 1], 0), PLANES - 1)
        delta_int, delta_sep = panel_solve(h_int, h_sep, leaf_inverse[panel], leaf_to_front[panel], front_to_leaf[panel], front_inverse[panel], live_all[panel])
        sol_int[panel] = fwd_int[panel] + delta_int
        sol_sep[panel] = fwd_sep[panel] + delta_sep
    return jnp.stack(sol_int), jnp.stack(sol_sep)
```

```python
import functools

import jax
import jax.numpy as jnp
from jax import lax
from jax.experimental import pallas as pl
from jax.experimental.pallas import tpu as pltpu
from jax.sharding import PartitionSpec as P

MESH = pl.DeviceIdType.MESH
F32, BF16 = jnp.float32, jnp.bfloat16
PORT = 256
PLANES = 4
SIDE = 4
GROUP = SIDE * SIDE
LEAF = 1024
SEP = 2560
OWN = SEP // GROUP
BLK = SEP // SIDE
SRC = 4
WIDE = 512


def hops(rel):
    return sum(min(d, SIDE - d) for d in divmod(rel, SIDE))


NEAR = sorted(range(GROUP), key=hops)
FAR = sorted(range(GROUP), key=lambda rel: -hops(rel))


def dot(lhs, rhs):
    return jnp.dot(lhs, rhs, preferred_element_type=F32)


def turned(vec):
    row = lax.broadcasted_iota(jnp.int32, vec.shape, 0)
    return jnp.where(row < SRC, -1.0, 1.0) * pltpu.roll(vec, SRC, axis=0)


def cmul(vec, w_re, w_im):
    return dot(vec.astype(BF16), w_re) + dot(turned(vec).astype(BF16), w_im)


def kernel(
    rint_ref, rsep_ref, fs_ref, l_hbm, a_hbm, c_hbm, f_hbm,
    oint_ref, osep_ref,
    lv, av, cv, fp, f2d, sel, selt, aaf, aab, naf, nab, aaf_nb, aab_nb, lq,
    inner_s, innerb_s, w_s, corr_s, f1_s, f_s, e_s, pre_s, is_s,
    base_src, fwd_src, bwd_src, f1_src, f2_src, uf_src, ub_src,
    base_rcv, fwd_rcv, bwd_rcv, f1_rcv, f2_rcv, uf_rcv, ub_rcv,
    load_sem, fp_send, fp_recv, aa_send, aa_recv, u_send, u_recv,
    base_send, base_recv, fwd_send, fwd_recv, bwd_send, bwd_recv,
    f1_send, f1_recv, f2_send, f2_recv,
):
    p, k = lax.axis_index("sweep"), lax.axis_index("leaf")
    last = lax.axis_size("sweep") - 1
    x, z = k // SIDE, lax.rem(k, SIDE)

    def to(rel):
        dx, dz = divmod(rel, SIDE)
        return lax.rem(x + dx, SIDE) * SIDE + lax.rem(z + dz, SIDE)

    def origin(rel):
        dx, dz = divmod(rel, SIDE)
        return lax.rem(x + SIDE - dx, SIDE) * SIDE + lax.rem(z + SIDE - dz, SIDE)

    loads = [
        pltpu.make_async_copy(l_hbm.at[0, 0], lv, load_sem.at[0]),
        pltpu.make_async_copy(a_hbm.at[0, 0], av, load_sem.at[1]),
        pltpu.make_async_copy(c_hbm.at[0, 0], cv, load_sem.at[2]),
        pltpu.make_async_copy(
            f_hbm.at[0, :, pl.ds(pl.multiple_of(z * BLK, BLK), BLK), :], fp.at[z], load_sem.at[3]
        ),
    ]
    for load in loads:
        load.start()

    barrier = pltpu.get_barrier_semaphore()
    for rel in range(1, GROUP):
        pl.semaphore_signal(barrier, inc=1, device_id={"leaf": to(rel)}, device_id_type=MESH)

    @pl.when(p < last)
    def _():
        for leaf in range(GROUP):
            pl.semaphore_signal(
                barrier, inc=1, device_id={"sweep": p + 1, "leaf": leaf}, device_id_type=MESH
            )

    @pl.when(p > 0)
    def _():
        for leaf in range(GROUP):
            pl.semaphore_signal(
                barrier, inc=1, device_id={"sweep": p - 1, "leaf": leaf}, device_id_type=MESH
            )

    @pl.when((p > 0) & (p < last))
    def _():
        pl.semaphore_wait(barrier, 3 * GROUP - 1)

    @pl.when((p == 0) | (p == last))
    def _():
        pl.semaphore_wait(barrier, 2 * GROUP - 1)

    def piece(dz):
        there = lax.rem(z + dz, SIDE)
        return pltpu.make_async_remote_copy(
            f_hbm.at[0, :, pl.ds(pl.multiple_of(there * BLK, BLK), BLK), :],
            fp.at[z],
            fp_send.at[dz],
            fp_recv.at[dz],
            device_id={"leaf": x * SIDE + there},
            device_id_type=MESH,
        )

    def piece_in(dz):
        here = lax.rem(z + SIDE - dz, SIDE)
        return pltpu.make_async_remote_copy(
            f_hbm.at[0, :, pl.ds(0, BLK), :],
            fp.at[here],
            fp_send.at[dz],
            fp_recv.at[dz],
            device_id={"leaf": x * SIDE + here},
            device_id_type=MESH,
        )

    for dz in range(1, SIDE):
        piece(dz).start()

    def out_copy(src, dst, send, recv, rel, slot, step):
        there = {"leaf": to(rel)}
        if step:
            there["sweep"] = p + step
        return pltpu.make_async_remote_copy(
            src.at[slot], dst.at[k], send.at[rel], recv.at[rel], device_id=there, device_id_type=MESH
        )

    def in_copy(src, dst, send, recv, rel, step):
        there = {"leaf": origin(rel)}
        if step:
            there["sweep"] = p - step
        return pltpu.make_async_remote_copy(
            src.at[0], dst.at[origin(rel)], send.at[rel], recv.at[rel],
            device_id=there, device_id_type=MESH,
        )

    def term_sends(src, dst, send, recv, step):
        return [
            out_copy(src, dst, send, recv, rel, SIDE if rel == 0 else lax.rem(to(rel), SIDE), step)
            for rel in FAR
            if step or rel
        ]

    def f_sends(src, dst, send, recv):
        return [out_copy(src, dst, send, recv, rel, 0, 0) for rel in FAR if rel]

    base_out = term_sends(base_src, base_rcv, base_send, base_recv, 0)
    fwd_out = term_sends(fwd_src, fwd_rcv, fwd_send, fwd_recv, 1)
    bwd_out = term_sends(bwd_src, bwd_rcv, bwd_send, bwd_recv, -1)
    f1_out = f_sends(f1_src, f1_rcv, f1_send, f1_recv)
    f2_out = f_sends(f2_src, f2_rcv, f2_send, f2_recv)

    def neighbour(src, dst, send, recv, step):
        return pltpu.make_async_remote_copy(
            src, dst, send, recv, device_id={"sweep": p + step}, device_id_type=MESH
        )

    aaf_out = neighbour(aaf, aaf_nb, aa_send.at[0], aa_recv.at[0], -1)
    aab_out = neighbour(aab, aab_nb, aa_send.at[1], aa_recv.at[1], 1)
    uf_out = neighbour(uf_src, uf_rcv, u_send.at[0], u_recv.at[0], 1)
    ub_out = neighbour(ub_src, ub_rcv, u_send.at[1], u_recv.at[1], -1)

    size = fs_ref[0, 0] + PORT
    col = lax.broadcasted_iota(jnp.int32, (1, LEAF), 1)
    live = jnp.where(col < size, 1.0, 0.0).astype(F32)

    def rows_of(ref):
        return jnp.concatenate([ref[0], ref[1]], axis=0)

    loads[0].wait()
    inner_s[...] = cmul(rows_of(rint_ref[0, 0]) * live, lv[0], lv[1])
    loads[1].wait()
    own = rows_of(rsep_ref[0]).astype(BF16)
    for blk in range(SIDE):
        cols = slice(blk * BLK, (blk + 1) * BLK)
        place = jnp.where(
            lax.broadcasted_iota(jnp.int32, (OWN, BLK), 1) + blk * BLK
            == lax.broadcasted_iota(jnp.int32, (OWN, BLK), 0) + k * OWN,
            1.0,
            0.0,
        ).astype(BF16)
        term = cmul(inner_s[:, :PORT], av[0, :, cols], av[1, :, cols]) - dot(own, place)
        base_src[blk] = term.astype(BF16)
    base_rcv[k] = base_src[z]
    for copy in base_out:
        copy.start()

    for at, plane in ((0, 0), (1, PLANES - 1)):
        cell = lax.broadcasted_iota(jnp.int32, (LEAF, PORT), 0)
        hit = (cell == lax.broadcasted_iota(jnp.int32, (LEAF, PORT), 1) * PLANES + plane) & (cell < size)
        sel[at] = jnp.where(hit, 1.0, 0.0).astype(BF16)
        cell = lax.broadcasted_iota(jnp.int32, (PORT, LEAF), 1)
        hit = (cell == lax.broadcasted_iota(jnp.int32, (PORT, LEAF), 0) * PLANES + plane) & (cell < size)
        selt[at] = jnp.where(hit, 1.0, 0.0).astype(BF16)

    def product(left_re, left_im, right, out):
        @pl.loop(0, SEP // WIDE)
        def _(i):
            cols = pl.ds(pl.multiple_of(i * WIDE, WIDE), WIDE)
            re, im = right[0, :, cols], right[1, :, cols]
            out[0, :, cols] = (dot(left_re, re) - dot(left_im, im)).astype(BF16)
            out[1, :, cols] = (dot(left_re, im) + dot(left_im, re)).astype(BF16)

    def picked(at):
        return (
            dot(selt[at], lv[0, :, :PORT]).astype(BF16),
            dot(selt[at], lv[1, :, :PORT]).astype(BF16),
        )

    @pl.when(p > 0)
    def _():
        left = picked(0)
        product(left[0], left[1], av, aaf)
        aaf_out.start()

    @pl.when(p < last)
    def _():
        left = picked(1)
        product(left[0], left[1], av, aab)
        aab_out.start()

    for at in range(2):
        for part in range(2):
            lq[at, part] = dot(lv[part, :PORT, :], sel[at]).astype(BF16)

    loads[3].wait()
    for dz in range(1, SIDE):
        piece_in(dz).wait_recv()
    for part in range(2):
        total = None
        for owner in range(SIDE):
            place = jnp.where(
                lax.broadcasted_iota(jnp.int32, (OWN, BLK), 1)
                == lax.broadcasted_iota(jnp.int32, (OWN, BLK), 0) + owner * OWN,
                1.0,
                0.0,
            ).astype(BF16)
            moved = dot(fp[owner, part], place)
            total = moved if total is None else total + moved
        f2d[part] = total.astype(BF16)
    loads[2].wait()

    def summed(src, dst, send, recv, step, total):
        for rel in NEAR:
            if step or rel:
                in_copy(src, dst, send, recv, rel, step).wait_recv()
            total = total + dst[origin(rel)].astype(F32)
        return total

    def ask(total, src, dst, out):
        part = cmul(-total, f2d[0], f2d[1]).astype(BF16)
        src[0] = part
        for copy in out:
            copy.start()
        dst[k] = part

    def answer(src, dst, send, recv):
        for rel in NEAR[1:]:
            in_copy(src, dst, send, recv, rel, 0).wait_recv()
        blocks = []
        for blk in range(SIDE):
            total = dst[blk * SIDE].astype(F32)
            for row in range(1, SIDE):
                total = total + dst[blk * SIDE + row].astype(F32)
            blocks.append(total)
        full = jnp.concatenate(blocks, axis=1)
        corr_s[...] = cmul(full, cv[0], cv[1])
        return full

    def keep(ref, full):
        for blk in range(SIDE):
            ref[blk] = full[:, blk * BLK : (blk + 1) * BLK]

    def shifted(blk, plane):
        lane = lax.rem(lax.broadcasted_iota(jnp.int32, blk.shape, 1), PLANES)
        only = jnp.where(lane == plane, blk, 0.0)
        return pltpu.roll(only, (BLK - PLANES + 1) if plane else (PLANES - 1), axis=1)

    def pass_on(na, src, out, plane, full_ref):
        for blk in range(SIDE):
            cols = slice(blk * BLK, (blk + 1) * BLK)
            src[blk] = (pre_s[:, cols] - cmul(corr_s[...], na[0, :, cols], na[1, :, cols])).astype(BF16)
        src[SIDE] = (src[z].astype(F32) - shifted(full_ref[z], plane)).astype(BF16)
        for copy in out:
            copy.start()

    def edge(at, src, copy):
        src[...] = (is_s[...] - cmul(corr_s[...], lq[at, 0], lq[at, 1])).astype(BF16)
        copy.start()

    def prepare(at, inner, aa):
        is_s[...] = dot(inner.astype(BF16), sel[at])
        pre_s[...] = cmul(is_s[...], aa[0], aa[1])

    def corrected(inner):
        return (inner - cmul(corr_s[...], lv[0, :PORT, :], lv[1, :PORT, :])) * live

    @pl.when(p > 0)
    def _():
        total = summed(base_src, base_rcv, base_send, base_recv, 0, jnp.zeros((2 * SRC, BLK), F32))
        total = summed(fwd_src, fwd_rcv, fwd_send, fwd_recv, 1, total)
        ask(total, f1_src, f1_rcv, f1_out)
        neighbour(uf_src, uf_rcv, u_send.at[0], u_recv.at[0], -1).wait_recv()
        spread = dot(uf_rcv[...], selt[0])
        inner_s[...] = inner_s[...] + cmul(spread, lv[0], lv[1])

    @pl.when(p == 0)
    def _():
        total = summed(base_src, base_rcv, base_send, base_recv, 0, jnp.zeros((2 * SRC, BLK), F32))
        ask(total, f1_src, f1_rcv, f1_out)

    @pl.when(p < last)
    def _():
        neighbour(aaf, aaf_nb, aa_send.at[0], aa_recv.at[0], 1).wait_recv()
        product(lq[1, 0], lq[1, 1], aaf_nb, naf)
        prepare(1, inner_s[...], aaf_nb)

    @pl.when(p > 0)
    def _():
        neighbour(aab, aab_nb, aa_send.at[1], aa_recv.at[1], -1).wait_recv()

    @pl.when(p == last)
    def _():
        product(lq[0, 0], lq[0, 1], aab_nb, nab)
        prepare(0, inner_s[...], aab_nb)

    keep(f1_s, answer(f1_src, f1_rcv, f1_send, f1_recv))

    @pl.when(p < last)
    def _():
        pass_on(naf, fwd_src, fwd_out, PLANES - 1, f1_s)
        edge(1, uf_src, uf_out)

    @pl.when(p == last)
    def _():
        pass_on(nab, bwd_src, bwd_out, 0, f1_s)
        edge(0, ub_src, ub_out)

    w_s[...] = corrected(inner_s[...])

    @pl.when((p > 0) & (p < last))
    def _():
        product(lq[0, 0], lq[0, 1], aab_nb, nab)

    @pl.when(p < last)
    def _():
        total = summed(bwd_src, bwd_rcv, bwd_send, bwd_recv, -1, jnp.zeros((2 * SRC, BLK), F32))
        ask(total, f2_src, f2_rcv, f2_out)
        neighbour(ub_src, ub_rcv, u_send.at[1], u_recv.at[1], 1).wait_recv()
        spread = dot(ub_rcv[...], selt[1])
        innerb_s[...] = cmul(spread, lv[0], lv[1])

    @pl.when((p > 0) & (p < last))
    def _():
        prepare(0, w_s[...] + innerb_s[...], aab_nb)

    @pl.when(p < last)
    def _():
        keep(f_s, answer(f2_src, f2_rcv, f2_send, f2_recv))
        for blk in range(SIDE):
            f1_s[blk] = f1_s[blk] + f_s[blk]

    @pl.when((p > 0) & (p < last))
    def _():
        pass_on(nab, bwd_src, bwd_out, 0, f1_s)
        edge(0, ub_src, ub_out)

    @pl.when(p < last)
    def _():
        w_s[...] = w_s[...] + corrected(innerb_s[...])

    oint_ref[0, 0, 0] = w_s[:SRC, :]
    oint_ref[0, 0, 1] = w_s[SRC:, :]
    block = f1_s[x]
    mine = jnp.zeros((2 * SRC, OWN), F32)
    for owner in range(SIDE):
        mine = jnp.where(z == owner, block[:, owner * OWN : (owner + 1) * OWN], mine)
    osep_ref[0, 0] = mine[:SRC]
    osep_ref[0, 1] = mine[SRC:]

    for dz in range(1, SIDE):
        piece(dz).wait_send()
    for copy in base_out + f1_out:
        copy.wait_send()

    @pl.when(p < last)
    def _():
        aab_out.wait_send()
        uf_out.wait_send()
        for copy in fwd_out + f2_out:
            copy.wait_send()

    @pl.when(p > 0)
    def _():
        aaf_out.wait_send()
        ub_out.wait_send()
        for copy in bwd_out:
            copy.wait_send()


def body(rhs_int, rhs_sep, leaf_inv, to_front, to_leaf, front_inv, sizes):
    vmem, anywhere = pl.BlockSpec(memory_space=pltpu.VMEM), pl.BlockSpec(memory_space=pl.ANY)
    rows = 2 * SRC

    def messages(count, width):
        return pltpu.VMEM((count, rows, width), BF16)

    scratch = [
        pltpu.VMEM((2, LEAF, LEAF), BF16),
        pltpu.VMEM((2, PORT, SEP), BF16),
        pltpu.VMEM((2, SEP, PORT), BF16),
        pltpu.VMEM((SIDE, 2, BLK, OWN), BF16),
        pltpu.VMEM((2, BLK, BLK), BF16),
        pltpu.VMEM((2, LEAF, PORT), BF16),
        pltpu.VMEM((2, PORT, LEAF), BF16),
    ]
    scratch += [pltpu.VMEM((2, PORT, SEP), BF16)] * 6
    scratch += [
        pltpu.VMEM((2, 2, PORT, PORT), BF16),
        pltpu.VMEM((rows, LEAF), F32),
        pltpu.VMEM((rows, LEAF), F32),
        pltpu.VMEM((rows, LEAF), F32),
        pltpu.VMEM((rows, PORT), F32),
        pltpu.VMEM((SIDE, rows, BLK), F32),
        pltpu.VMEM((SIDE, rows, BLK), F32),
        pltpu.VMEM((SIDE, rows, BLK), F32),
        pltpu.VMEM((rows, SEP), F32),
        pltpu.VMEM((rows, PORT), F32),
    ]
    scratch += [messages(SIDE + 1, BLK)] * 3 + [messages(1, BLK)] * 2
    scratch += [pltpu.VMEM((rows, PORT), BF16)] * 2
    scratch += [messages(GROUP, BLK)] * 5 + [pltpu.VMEM((rows, PORT), BF16)] * 2
    dma = pltpu.SemaphoreType.DMA
    scratch += [dma((4,)), dma((SIDE,)), dma((SIDE,))] + [dma((2,))] * 4 + [dma((GROUP,))] * 10
    return pl.pallas_call(
        kernel,
        out_shape=(
            jax.ShapeDtypeStruct(rhs_int.shape, F32),
            jax.ShapeDtypeStruct(rhs_sep.shape, F32),
        ),
        in_specs=[vmem, vmem, pl.BlockSpec(memory_space=pltpu.SMEM)] + [anywhere] * 4,
        out_specs=(vmem, vmem),
        scratch_shapes=scratch,
        compiler_params=pltpu.CompilerParams(
            collective_id=0, has_side_effects=True, vmem_limit_bytes=60 << 20
        ),
    )(rhs_int, rhs_sep, sizes, leaf_inv, to_front, to_leaf, front_inv)


def solution(mesh):
    placed = (
        P("sweep", "leaf", None, None, None),
        P("sweep", None, None, "leaf"),
        P("sweep", "leaf", None, None, None),
        P("sweep", "leaf", None, None, None),
        P("sweep", "leaf", None, None, None),
        P("sweep", None, None, "leaf"),
        P("sweep", "leaf"),
    )
    return jax.shard_map(
        body,
        mesh=mesh,
        in_specs=placed,
        out_specs=(P("sweep", "leaf", None, None, None), P("sweep", None, None, "leaf")),
        check_vma=False,
    )
```

```python
import functools

import jax
import jax.numpy as jnp
from jax import lax
from jax.experimental import pallas as pl
from jax.experimental.pallas import tpu as pltpu
from jax.sharding import PartitionSpec as P

MESH = pl.DeviceIdType.MESH
F32, BF16 = jnp.float32, jnp.bfloat16
PORT = 256
PLANES = 4
SIDE = 4
GROUP = SIDE * SIDE
LEAF = 1024
SEP = 2560
OWN = SEP // GROUP
BLK = SEP // SIDE
SRC = 4
CALLER = 1
WIDE = 512


def hops(rel):
    return sum(min(d, SIDE - d) for d in divmod(rel, SIDE))


NEAR = sorted(range(GROUP), key=hops)
FAR = sorted(range(GROUP), key=lambda rel: -hops(rel))
AWAY = (2, 1, 3, 0)


def dot(lhs, rhs):
    return jnp.dot(lhs, rhs, preferred_element_type=F32)


def dot_t(lhs, rhs):
    return lax.dot_general(lhs, rhs, (((1,), (1,)), ((), ())), preferred_element_type=F32)


def turned(vec):
    row = lax.broadcasted_iota(jnp.int32, vec.shape, 0)
    return jnp.where(row < SRC, -1.0, 1.0) * pltpu.roll(vec, SRC, axis=0)


def cmul(vec, w_re, w_im):
    return dot(vec.astype(BF16), w_re) + dot(turned(vec).astype(BF16), w_im)


def kernel(
    rint_ref, rsep_ref, fs_ref, l_hbm, a_hbm, c_hbm, f_hbm,
    oint_ref, osep_ref,
    lv, av, cv, fo, f2t, f2d, place, sel, selt, aaf, aab, naf, nab, aaf_nb, aab_nb, lq,
    inner_s, innerb_s, w_s, corr_s, f1_s, pre_s, is_s,
    all_src, base_src, fwd_src, bwd_src, own_src, f1_src, f2_src, uf_src, ub_src,
    all_rcv, base_rcv, fwd_rcv, bwd_rcv, f1_rcv, f2_rcv, uf_rcv, ub_rcv,
    go_sem, turn_sem, load_sem, fp_send, fp_recv, aa_send, aa_recv, u_send, u_recv,
    base_send, base_recv, fwd_send, fwd_recv, bwd_send, bwd_recv,
    own_send, f1_send, f1_recv, f2_send, f2_recv,
):
    p, k = lax.axis_index("sweep"), lax.axis_index("leaf")
    last = lax.axis_size("sweep") - 1
    x, z = k // SIDE, lax.rem(k, SIDE)

    def to(rel):
        dx, dz = divmod(rel, SIDE)
        return lax.rem(x + dx, SIDE) * SIDE + lax.rem(z + dz, SIDE)

    def origin(rel):
        dx, dz = divmod(rel, SIDE)
        return lax.rem(x + SIDE - dx, SIDE) * SIDE + lax.rem(z + SIDE - dz, SIDE)

    def block_of(side):
        return pl.ds(pl.multiple_of(side * BLK, BLK), BLK)

    def owned_by(side):
        return pl.ds(pl.multiple_of(side * OWN, OWN), OWN)

    loads = [
        pltpu.make_async_copy(l_hbm.at[0, 0], lv, load_sem.at[0]),
        pltpu.make_async_copy(a_hbm.at[0, 0], av, load_sem.at[1]),
        pltpu.make_async_copy(c_hbm.at[0, 0], cv, load_sem.at[2]),
        pltpu.make_async_copy(
            f_hbm.at[0, :, :, block_of(z)], f2t.at[:, owned_by(z), :], load_sem.at[3]
        ),
    ]
    for load in loads:
        load.start()
    whole = pltpu.make_async_copy(f_hbm.at[0], fo, load_sem.at[4])

    @pl.when(p == 0)
    def _():
        whole.start()

    barrier = pltpu.get_barrier_semaphore()
    for rel in range(1, GROUP):
        pl.semaphore_signal(barrier, inc=1, device_id={"leaf": to(rel)}, device_id_type=MESH)

    @pl.when(p < last)
    def _():
        for leaf in range(GROUP):
            pl.semaphore_signal(
                barrier, inc=1, device_id={"sweep": p + 1, "leaf": leaf}, device_id_type=MESH
            )

    @pl.when(p > 0)
    def _():
        for leaf in range(GROUP):
            pl.semaphore_signal(
                barrier, inc=1, device_id={"sweep": p - 1, "leaf": leaf}, device_id_type=MESH
            )

    size = fs_ref[0, 0] + PORT
    for at, plane in ((0, 0), (1, PLANES - 1)):
        cell = lax.broadcasted_iota(jnp.int32, (LEAF, PORT), 0)
        hit = (cell == lax.broadcasted_iota(jnp.int32, (LEAF, PORT), 1) * PLANES + plane) & (cell < size)
        sel[at] = jnp.where(hit, 1.0, 0.0).astype(BF16)
        cell = lax.broadcasted_iota(jnp.int32, (PORT, LEAF), 1)
        hit = (cell == lax.broadcasted_iota(jnp.int32, (PORT, LEAF), 0) * PLANES + plane) & (cell < size)
        selt[at] = jnp.where(hit, 1.0, 0.0).astype(BF16)

    for blk in range(SIDE):
        hit = (
            lax.broadcasted_iota(jnp.int32, (OWN, BLK), 1) + blk * BLK
            == lax.broadcasted_iota(jnp.int32, (OWN, BLK), 0) + k * OWN
        )
        place[blk] = jnp.where(hit, 1.0, 0.0).astype(BF16)

    @pl.when((p > 0) & (p < last))
    def _():
        pl.semaphore_wait(barrier, 3 * GROUP - 1)

    @pl.when((p == 0) | (p == last))
    def _():
        pl.semaphore_wait(barrier, 2 * GROUP - 1)

    def piece(dz):
        there = lax.rem(z + dz, SIDE)
        return pltpu.make_async_remote_copy(
            f_hbm.at[0, :, :, block_of(there)],
            f2t.at[:, owned_by(z), :],
            fp_send.at[dz],
            fp_recv.at[dz],
            device_id={"leaf": x * SIDE + there},
            device_id_type=MESH,
        )

    def piece_in(dz):
        here = lax.rem(z + SIDE - dz, SIDE)
        return pltpu.make_async_remote_copy(
            f_hbm.at[0, :, :, block_of(z)],
            f2t.at[:, owned_by(here), :],
            fp_send.at[dz],
            fp_recv.at[dz],
            device_id={"leaf": x * SIDE + here},
            device_id_type=MESH,
        )

    first = lax.rem(p, 2) == 1

    @pl.when(first)
    def _():
        for dz in (1, SIDE - 1):
            piece(dz).start()

    def let_go():
        pl.semaphore_signal(go_sem, inc=1, device_id={"sweep": p + 1}, device_id_type=MESH)

    @pl.when(jnp.logical_not(first) & (p > 0))
    def _():
        let_go()

    def out_copy(src, dst, send, recv, rel, slot, step):
        there = {"leaf": to(rel)}
        if step:
            there["sweep"] = p + step
        return pltpu.make_async_remote_copy(
            src.at[slot], dst.at[k], send.at[rel], recv.at[rel], device_id=there, device_id_type=MESH
        )

    def in_copy(src, dst, send, recv, rel, step):
        there = {"leaf": origin(rel)}
        if step:
            there["sweep"] = p - step
        return pltpu.make_async_remote_copy(
            src.at[0], dst.at[origin(rel)], send.at[rel], recv.at[rel],
            device_id=there, device_id_type=MESH,
        )

    def term_sends(src, dst, send, recv, step):
        return {
            dz: [
                out_copy(
                    src, dst, send, recv, dx * SIDE + dz,
                    SIDE if dx == dz == 0 else lax.rem(z + dz, SIDE), step,
                )
                for dx in AWAY
                if step or dx or dz
            ]
            for dz in AWAY
        }

    def f_sends(src, dst, send, recv):
        return [out_copy(src, dst, send, recv, rel, 0, 0) for rel in FAR if rel]

    narrow = f1_src.at[:, :, :PORT], f1_rcv.at[:, :, :PORT]

    base_out = term_sends(base_src, base_rcv, base_send, base_recv, 0)
    all_out = f_sends(all_src, all_rcv, base_send, base_recv)
    own_out = term_sends(own_src, fwd_rcv, own_send, fwd_recv, 0)
    f0_out = f_sends(*narrow, f1_send, f1_recv)
    fwd_out = term_sends(fwd_src, fwd_rcv, fwd_send, fwd_recv, 1)
    bwd_out = term_sends(bwd_src, bwd_rcv, bwd_send, bwd_recv, -1)
    f1_out = f_sends(f1_src, f1_rcv, f1_send, f1_recv)
    f2_out = f_sends(f2_src, f2_rcv, f2_send, f2_recv)

    def flat(sends):
        return [copy for dz in AWAY for copy in sends[dz]]

    def neighbour(src, dst, send, recv, step):
        return pltpu.make_async_remote_copy(
            src, dst, send, recv, device_id={"sweep": p + step}, device_id_type=MESH
        )

    aaf_out = neighbour(aaf, aaf_nb, aa_send.at[0], aa_recv.at[0], -1)
    aab_out = neighbour(aab, aab_nb, aa_send.at[1], aa_recv.at[1], 1)
    uf_out = neighbour(uf_src, uf_rcv, u_send.at[0], u_recv.at[0], 1)
    ub_out = neighbour(ub_src, ub_rcv, u_send.at[1], u_recv.at[1], -1)

    col = lax.broadcasted_iota(jnp.int32, (1, LEAF), 1)
    live = jnp.where(col < size, 1.0, 0.0).astype(F32)

    def rows_of(ref):
        return jnp.concatenate([ref[0], ref[1]], axis=0)

    loads[0].wait()
    inner_s[...] = cmul(rows_of(rint_ref[0, 0]) * live, lv[0], lv[1])
    loads[1].wait()
    own = rows_of(rsep_ref[0]).astype(BF16)
    for blk in range(SIDE):
        cols = slice(blk * BLK, (blk + 1) * BLK)
        term = cmul(inner_s[:, :PORT], av[0, :, cols], av[1, :, cols]) - dot(own, place[blk])
        base_src[blk] = term.astype(BF16)
        all_src[0, :, cols] = term.astype(BF16)

    @pl.when(p == 0)
    def _():
        for copy in all_out:
            copy.start()

    @pl.when(p > 0)
    def _():
        for copy in flat(base_out):
            copy.start()
        base_rcv[k] = base_src[z]

    @pl.when(p == 0)
    def _():
        all_rcv[k] = all_src[0]


    def product(left_re, left_im, right, out):
        @pl.loop(0, SEP // WIDE)
        def _(i):
            cols = pl.ds(pl.multiple_of(i * WIDE, WIDE), WIDE)
            re, im = right[0, :, cols], right[1, :, cols]
            out[0, :, cols] = (dot(left_re, re) - dot(left_im, im)).astype(BF16)
            out[1, :, cols] = (dot(left_re, im) + dot(left_im, re)).astype(BF16)

    def picked(at):
        return (
            dot(selt[at], lv[0, :, :PORT]).astype(BF16),
            dot(selt[at], lv[1, :, :PORT]).astype(BF16),
        )

    @pl.when(p > 0)
    def _():
        left = picked(0)
        product(left[0], left[1], av, aaf)

    @pl.when((p > 0) & (p != CALLER + 1))
    def _():
        aaf_out.start()

    def give_back():
        left = picked(1)
        product(left[0], left[1], av, aab)
        aab_out.start()

    @pl.when((p > CALLER) & (p < last))
    def _():
        give_back()

    for at in range(2):
        for part in range(2):
            lq[at, part] = dot(lv[part, :PORT, :], sel[at]).astype(BF16)

    def resplit():
        @pl.when(first)
        def _():
            pl.semaphore_wait(go_sem, 1)
            piece(2).start()

        @pl.when(jnp.logical_not(first))
        def _():
            pl.semaphore_wait(turn_sem, 1)
            for dz in range(1, SIDE):
                piece(dz).start()

        loads[3].wait()
        for dz in range(1, SIDE):
            piece_in(dz).wait_recv()

        @pl.when(first)
        def _():
            pl.semaphore_signal(turn_sem, inc=1, device_id={"sweep": p - 1}, device_id_type=MESH)

        for part in range(2):
            f2d[part] = f2t[part].T

    @pl.when(p > 0)
    def _():
        resplit()

    loads[2].wait()

    def summed(src, dst, send, recv, step, total):
        for rel in NEAR:
            if step or rel:
                in_copy(src, dst, send, recv, rel, step).wait_recv()
            total = total + dst[origin(rel)].astype(F32)
        return total

    def ask(total, src, dst, out):
        part = cmul(-total, f2d[0], f2d[1]).astype(BF16)
        src[0] = part
        for copy in out:
            copy.start()
        dst[k] = part

    def answer(src, dst, send, recv, old, pieces):
        corr = jnp.zeros((2 * SRC, PORT), F32)
        for dx in reversed(AWAY):
            blk = lax.rem(x + SIDE - dx, SIDE)
            for dz in reversed(AWAY):
                if dx or dz:
                    in_copy(src, dst, send, recv, dx * SIDE + dz, 0).wait_recv()
            parts = [dst[blk * SIDE + row].astype(F32) for row in range(SIDE)]
            if pieces:
                total = jnp.concatenate([part[:, :OWN] for part in parts], axis=1)
            else:
                total = (parts[0] + parts[1]) + (parts[2] + parts[3])
            rows = block_of(blk)
            corr = corr + cmul(total, cv[0, rows, :], cv[1, rows, :])
            f1_s[blk] = f1_s[blk] + total if old else total
        corr_s[...] = corr

    def shifted(blk, plane):
        lane = lax.rem(lax.broadcasted_iota(jnp.int32, blk.shape, 1), PLANES)
        only = jnp.where(lane == plane, blk, 0.0)
        return pltpu.roll(only, (BLK - PLANES + 1) if plane else (PLANES - 1), axis=1)

    def pass_on(na, src, out, plane):
        for dz in AWAY:
            at = lax.rem(z + dz, SIDE)
            cols = block_of(at)
            term = pre_s[at] - cmul(corr_s[...], na[0, :, cols], na[1, :, cols])
            src[at] = term.astype(BF16)
            if dz == 0:
                src[SIDE] = (term - shifted(f1_s[at], plane)).astype(BF16)
            for copy in out[dz]:
                copy.start()

    def edge(at, plane, src, copy):
        src[:, :PORT] = (is_s[...] - cmul(corr_s[...], lq[at, 0], lq[at, 1])).astype(BF16)
        src[:, PORT:] = shifted(f1_s[z], plane).astype(BF16)
        copy.start()

    def prepare(at, inner, aa):
        is_s[...] = dot(inner.astype(BF16), sel[at])
        for blk in range(SIDE):
            cols = slice(blk * BLK, (blk + 1) * BLK)
            pre_s[blk] = cmul(is_s[...], aa[0, :, cols], aa[1, :, cols])

    def corrected(inner):
        return (inner - cmul(corr_s[...], lv[0, :PORT, :], lv[1, :PORT, :])) * live

    zero = jnp.zeros((2 * SRC, BLK), F32)

    def take_edge():
        neighbour(uf_src, uf_rcv, u_send.at[0], u_recv.at[0], -1).wait_recv()

    def take_inner():
        spread = dot(uf_rcv[:, :PORT], selt[0])
        inner_s[...] = inner_s[...] + cmul(spread, lv[0], lv[1])

    @pl.when(p == 0)
    def _():
        total = all_rcv[k].astype(F32)
        for rel in NEAR[1:]:
            in_copy(all_src, all_rcv, base_send, base_recv, rel, 0).wait_recv()
            total = total + all_rcv[origin(rel)].astype(F32)
        let_go()
        whole.wait()
        minus = -total
        part = dot_t(minus.astype(BF16), fo[0]) + dot_t(turned(minus).astype(BF16), fo[1])
        f1_src[0, :, :OWN] = part.astype(BF16)
        for copy in f0_out:
            copy.start()
        f1_rcv[k, :, :OWN] = part.astype(BF16)

    @pl.when((p > 0) & (p != CALLER + 1))
    def _():
        total = summed(base_src, base_rcv, base_send, base_recv, 0, zero)
        total = summed(fwd_src, fwd_rcv, fwd_send, fwd_recv, 1, total)
        ask(total, f1_src, f1_rcv, f1_out)
        take_edge()
        take_inner()

    @pl.when(p == CALLER + 1)
    def _():
        total = summed(base_src, base_rcv, base_send, base_recv, 0, zero)
        take_edge()
        for dz in AWAY:
            at = lax.rem(z + dz, SIDE)
            cols = block_of(at)
            term = cmul(uf_rcv[:, :PORT].astype(F32), aaf[0, :, cols], aaf[1, :, cols])
            own_src[at] = term.astype(BF16)
            for copy in own_out[dz]:
                copy.start()
        fwd_rcv[k] = (own_src[z].astype(F32) - uf_rcv[:, PORT:].astype(F32)).astype(BF16)
        total = summed(own_src, fwd_rcv, own_send, fwd_recv, 0, total)
        ask(total, f1_src, f1_rcv, f1_out)
        take_inner()

    @pl.when(p == CALLER)
    def _():
        is_s[...] = dot(inner_s[...].astype(BF16), sel[1])

    @pl.when((p < last) & (p != CALLER))
    def _():
        neighbour(aaf, aaf_nb, aa_send.at[0], aa_recv.at[0], 1).wait_recv()
        product(lq[1, 0], lq[1, 1], aaf_nb, naf)
        prepare(1, inner_s[...], aaf_nb)

    def take_back():
        neighbour(aab, aab_nb, aa_send.at[1], aa_recv.at[1], -1).wait_recv()
        product(lq[0, 0], lq[0, 1], aab_nb, nab)

    @pl.when(p == last)
    def _():
        take_back()
        prepare(0, inner_s[...], aab_nb)

    @pl.when(p == 0)
    def _():
        answer(*narrow, f1_send, f1_recv, False, True)

    @pl.when(p > 0)
    def _():
        answer(f1_src, f1_rcv, f1_send, f1_recv, False, False)


    @pl.when((p < last) & (p != CALLER))
    def _():
        pass_on(naf, fwd_src, fwd_out, PLANES - 1)

    @pl.when(p < last)
    def _():
        edge(1, PLANES - 1, uf_src, uf_out)

    @pl.when(p == last)
    def _():
        pass_on(nab, bwd_src, bwd_out, 0)
        edge(0, 0, ub_src, ub_out)

    w_s[...] = corrected(inner_s[...])

    @pl.when(p == 0)
    def _():
        resplit()

    @pl.when(p <= CALLER)
    def _():
        give_back()

    @pl.when((p > 0) & (p < last))
    def _():
        take_back()

    @pl.when(p < last)
    def _():
        total = summed(bwd_src, bwd_rcv, bwd_send, bwd_recv, -1, zero)
        ask(total, f2_src, f2_rcv, f2_out)
        neighbour(ub_src, ub_rcv, u_send.at[1], u_recv.at[1], 1).wait_recv()
        spread = dot(ub_rcv[:, :PORT], selt[1])
        innerb_s[...] = cmul(spread, lv[0], lv[1])

    @pl.when((p > 0) & (p < last))
    def _():
        prepare(0, w_s[...] + innerb_s[...], aab_nb)

    @pl.when(p < last)
    def _():
        answer(f2_src, f2_rcv, f2_send, f2_recv, True, False)

    @pl.when((p > 0) & (p < last))
    def _():
        pass_on(nab, bwd_src, bwd_out, 0)
        edge(0, 0, ub_src, ub_out)

    @pl.when(p < last)
    def _():
        w_s[...] = w_s[...] + corrected(innerb_s[...])

    oint_ref[0, 0, 0] = w_s[:SRC, :]
    oint_ref[0, 0, 1] = w_s[SRC:, :]
    block = f1_s[x]
    mine = jnp.zeros((2 * SRC, OWN), F32)
    for owner in range(SIDE):
        mine = jnp.where(z == owner, block[:, owner * OWN : (owner + 1) * OWN], mine)
    osep_ref[0, 0] = mine[:SRC]
    osep_ref[0, 1] = mine[SRC:]

    for dz in range(1, SIDE):
        piece(dz).wait_send()

    @pl.when(p == 0)
    def _():
        for copy in all_out + f0_out:
            copy.wait_send()

    @pl.when(p > 0)
    def _():
        for copy in flat(base_out) + f1_out + flat(bwd_out):
            copy.wait_send()
        ub_out.wait_send()

    @pl.when((p > 0) & (p != CALLER + 1))
    def _():
        aaf_out.wait_send()

    @pl.when(p == CALLER + 1)
    def _():
        for copy in flat(own_out):
            copy.wait_send()

    @pl.when(p < last)
    def _():
        aab_out.wait_send()
        uf_out.wait_send()
        for copy in f2_out:
            copy.wait_send()

    @pl.when((p < last) & (p != CALLER))
    def _():
        for copy in flat(fwd_out):
            copy.wait_send()


def body(rhs_int, rhs_sep, leaf_inv, to_front, to_leaf, front_inv, sizes):
    vmem, anywhere = pl.BlockSpec(memory_space=pltpu.VMEM), pl.BlockSpec(memory_space=pl.ANY)
    rows = 2 * SRC

    def messages(count, width):
        return pltpu.VMEM((count, rows, width), BF16)

    scratch = [
        pltpu.VMEM((2, LEAF, LEAF), BF16),
        pltpu.VMEM((2, PORT, SEP), BF16),
        pltpu.VMEM((2, SEP, PORT), BF16),
        pltpu.VMEM((2, OWN, SEP), BF16),
        pltpu.VMEM((2, BLK, BLK), BF16),
        pltpu.VMEM((2, BLK, BLK), BF16),
        pltpu.VMEM((SIDE, OWN, BLK), BF16),
        pltpu.VMEM((2, LEAF, PORT), BF16),
        pltpu.VMEM((2, PORT, LEAF), BF16),
    ]
    scratch += [pltpu.VMEM((2, PORT, SEP), BF16)] * 6
    scratch += [
        pltpu.VMEM((2, 2, PORT, PORT), BF16),
        pltpu.VMEM((rows, LEAF), F32),
        pltpu.VMEM((rows, LEAF), F32),
        pltpu.VMEM((rows, LEAF), F32),
        pltpu.VMEM((rows, PORT), F32),
        pltpu.VMEM((SIDE, rows, BLK), F32),
        pltpu.VMEM((SIDE, rows, BLK), F32),
        pltpu.VMEM((rows, PORT), F32),
    ]
    scratch += [messages(1, SEP)] + [messages(SIDE + 1, BLK)] * 4 + [messages(1, BLK)] * 2
    scratch += [pltpu.VMEM((rows, PORT + BLK), BF16)] * 2
    scratch += [messages(GROUP, SEP)] + [messages(GROUP, BLK)] * 5 + [pltpu.VMEM((rows, PORT + BLK), BF16)] * 2
    dma = pltpu.SemaphoreType.DMA
    scratch += [pltpu.SemaphoreType.REGULAR] * 2 + [dma((5,)), dma((SIDE,)), dma((SIDE,))] + [dma((2,))] * 4 + [dma((GROUP,))] * 11
    return pl.pallas_call(
        kernel,
        out_shape=(
            jax.ShapeDtypeStruct(rhs_int.shape, F32),
            jax.ShapeDtypeStruct(rhs_sep.shape, F32),
        ),
        in_specs=[vmem, vmem, pl.BlockSpec(memory_space=pltpu.SMEM)] + [anywhere] * 4,
        out_specs=(vmem, vmem),
        scratch_shapes=scratch,
        compiler_params=pltpu.CompilerParams(
            collective_id=0, has_side_effects=True, vmem_limit_bytes=60 << 20
        ),
    )(rhs_int, rhs_sep, sizes, leaf_inv, to_front, to_leaf, front_inv.swapaxes(2, 3))


def solution(mesh):
    placed = (
        P("sweep", "leaf", None, None, None),
        P("sweep", None, None, "leaf"),
        P("sweep", "leaf", None, None, None),
        P("sweep", "leaf", None, None, None),
        P("sweep", "leaf", None, None, None),
        P("sweep", None, None, "leaf"),
        P("sweep", "leaf"),
    )
    return jax.shard_map(
        body,
        mesh=mesh,
        in_specs=placed,
        out_specs=(P("sweep", "leaf", None, None, None), P("sweep", None, None, "leaf")),
        check_vma=False,
    )
```

```python
import functools

import jax
import jax.numpy as jnp
from jax import lax
from jax.experimental import pallas as pl
from jax.experimental.pallas import tpu as pltpu
from jax.sharding import PartitionSpec as P

MESH = pl.DeviceIdType.MESH
F32, BF16 = jnp.float32, jnp.bfloat16
PORT = 256
PLANES = 4
SIDE = 4
GROUP = SIDE * SIDE
LEAF = 1024
SEP = 2560
OWN = SEP // GROUP
BLK = SEP // SIDE
SRC = 4
CALLER = 1
WIDE = 512


def hops(rel):
    return sum(min(d, SIDE - d) for d in divmod(rel, SIDE))


NEAR = sorted(range(GROUP), key=hops)
FAR = sorted(range(GROUP), key=lambda rel: -hops(rel))
AWAY = (2, 1, 3, 0)


def dot(lhs, rhs):
    return jnp.dot(lhs, rhs, preferred_element_type=F32)


def dot_t(lhs, rhs):
    return lax.dot_general(lhs, rhs, (((1,), (1,)), ((), ())), preferred_element_type=F32)


def turned(vec):
    row = lax.broadcasted_iota(jnp.int32, vec.shape, 0)
    return jnp.where(row < SRC, -1.0, 1.0) * pltpu.roll(vec, SRC, axis=0)


def cmul(vec, w_re, w_im):
    return dot(vec.astype(BF16), w_re) + dot(turned(vec).astype(BF16), w_im)


def kernel(
    rint_hbm, rsep_hbm, fs_ref, l_hbm, a_hbm, c_hbm, f_hbm,
    oint_ref, osep_ref,
    rint_ref, rsep_ref, lv, av, cv, fo, f2t, f2d, place, sel, selt, aaf, aab, naf, nab, aaf_nb, aab_nb, lq,
    inner_s, innerb_s, w_s, corr_s, f1_s, pre_s, is_s,
    base_src, fwd_src, bwd_src, own_src, f1_src, f2_src, uf_src, ub_src, q_rcv,
    base_rcv, fwd_rcv, bwd_rcv, f1_rcv, f2_rcv, uf_rcv, ub_rcv,
    go_sem, turn_sem, load_sem, q_send, q_recv, fp_send, fp_recv, aa_send, aa_recv, u_send, u_recv,
    base_send, base_recv, fwd_send, fwd_recv, bwd_send, bwd_recv,
    own_send, f1_send, f1_recv, f2_send, f2_recv,
):
    p, k = lax.axis_index("sweep"), lax.axis_index("leaf")
    last = lax.axis_size("sweep") - 1
    x, z = k // SIDE, lax.rem(k, SIDE)

    def to(rel):
        dx, dz = divmod(rel, SIDE)
        return lax.rem(x + dx, SIDE) * SIDE + lax.rem(z + dz, SIDE)

    def origin(rel):
        dx, dz = divmod(rel, SIDE)
        return lax.rem(x + SIDE - dx, SIDE) * SIDE + lax.rem(z + SIDE - dz, SIDE)

    def block_of(side):
        return pl.ds(pl.multiple_of(side * BLK, BLK), BLK)

    def owned_by(side):
        return pl.ds(pl.multiple_of(side * OWN, OWN), OWN)

    early = [
        pltpu.make_async_copy(rint_hbm.at[0, 0], rint_ref, load_sem.at[0]),
        pltpu.make_async_copy(l_hbm.at[0, 0], lv, load_sem.at[1]),
        pltpu.make_async_copy(rsep_hbm.at[0], rsep_ref, load_sem.at[2]),
        pltpu.make_async_copy(a_hbm.at[0, 0], av, load_sem.at[3]),
    ]
    late = [
        pltpu.make_async_copy(c_hbm.at[0, 0], cv, load_sem.at[4]),
        pltpu.make_async_copy(
            f_hbm.at[0, :, :, block_of(z)], f2t.at[:, owned_by(z), :], load_sem.at[5]
        ),
    ]
    whole = pltpu.make_async_copy(f_hbm.at[0], fo, load_sem.at[6])
    for load in early:
        load.start()

    barrier = pltpu.get_barrier_semaphore()
    for rel in range(1, GROUP):
        pl.semaphore_signal(barrier, inc=1, device_id={"leaf": to(rel)}, device_id_type=MESH)

    @pl.when(p < last)
    def _():
        for leaf in range(GROUP):
            pl.semaphore_signal(
                barrier, inc=1, device_id={"sweep": p + 1, "leaf": leaf}, device_id_type=MESH
            )

    @pl.when(p > 0)
    def _():
        for leaf in range(GROUP):
            pl.semaphore_signal(
                barrier, inc=1, device_id={"sweep": p - 1, "leaf": leaf}, device_id_type=MESH
            )

    size = fs_ref[0, 0] + PORT
    for at, plane in ((0, 0), (1, PLANES - 1)):
        cell = lax.broadcasted_iota(jnp.int32, (LEAF, PORT), 0)
        hit = (cell == lax.broadcasted_iota(jnp.int32, (LEAF, PORT), 1) * PLANES + plane) & (cell < size)
        sel[at] = jnp.where(hit, 1.0, 0.0).astype(BF16)
        cell = lax.broadcasted_iota(jnp.int32, (PORT, LEAF), 1)
        hit = (cell == lax.broadcasted_iota(jnp.int32, (PORT, LEAF), 0) * PLANES + plane) & (cell < size)
        selt[at] = jnp.where(hit, 1.0, 0.0).astype(BF16)

    for blk in range(SIDE):
        hit = (
            lax.broadcasted_iota(jnp.int32, (OWN, BLK), 1) + blk * BLK
            == lax.broadcasted_iota(jnp.int32, (OWN, BLK), 0) + k * OWN
        )
        place[blk] = jnp.where(hit, 1.0, 0.0).astype(BF16)

    col = lax.broadcasted_iota(jnp.int32, (1, LEAF), 1)
    live = jnp.where(col < size, 1.0, 0.0).astype(F32)

    def rows_of(ref):
        return jnp.concatenate([ref[0], ref[1]], axis=0)

    early[0].wait()
    early[1].wait()
    inner_s[...] = cmul(rows_of(rint_ref) * live, lv[0], lv[1])
    early[2].wait()
    early[3].wait()
    own = rows_of(rsep_ref).astype(BF16)
    for blk in range(SIDE):
        cols = slice(blk * BLK, (blk + 1) * BLK)
        term = cmul(inner_s[:, :PORT], av[0, :, cols], av[1, :, cols]) - dot(own, place[blk])
        base_src[blk] = term.astype(BF16)

    @pl.when((p > 0) & (p < last))
    def _():
        pl.semaphore_wait(barrier, 3 * GROUP - 1)

    @pl.when((p == 0) | (p == last))
    def _():
        pl.semaphore_wait(barrier, 2 * GROUP - 1)

    def piece(dz):
        there = lax.rem(z + dz, SIDE)
        return pltpu.make_async_remote_copy(
            f_hbm.at[0, :, :, block_of(there)],
            f2t.at[:, owned_by(z), :],
            fp_send.at[dz],
            fp_recv.at[dz],
            device_id={"leaf": x * SIDE + there},
            device_id_type=MESH,
        )

    def piece_in(dz):
        here = lax.rem(z + SIDE - dz, SIDE)
        return pltpu.make_async_remote_copy(
            f_hbm.at[0, :, :, block_of(z)],
            f2t.at[:, owned_by(here), :],
            fp_send.at[dz],
            fp_recv.at[dz],
            device_id={"leaf": x * SIDE + here},
            device_id_type=MESH,
        )

    first = lax.rem(p, 2) == 1

    @pl.when(first)
    def _():
        for dz in (1, SIDE - 1):
            piece(dz).start()

    def let_go():
        pl.semaphore_signal(go_sem, inc=1, device_id={"sweep": p + 1}, device_id_type=MESH)

    @pl.when(jnp.logical_not(first) & (p > 0))
    def _():
        let_go()

    def out_copy(src, dst, send, recv, rel, slot, step):
        there = {"leaf": to(rel)}
        if step:
            there["sweep"] = p + step
        return pltpu.make_async_remote_copy(
            src.at[slot], dst.at[k], send.at[rel], recv.at[rel], device_id=there, device_id_type=MESH
        )

    def in_copy(src, dst, send, recv, rel, step):
        there = {"leaf": origin(rel)}
        if step:
            there["sweep"] = p - step
        return pltpu.make_async_remote_copy(
            src.at[0], dst.at[origin(rel)], send.at[rel], recv.at[rel],
            device_id=there, device_id_type=MESH,
        )

    def term_sends(src, dst, send, recv, step):
        return {
            dz: [
                out_copy(
                    src, dst, send, recv, dx * SIDE + dz,
                    SIDE if dx == dz == 0 else lax.rem(z + dz, SIDE), step,
                )
                for dx in AWAY
                if step or dx or dz
            ]
            for dz in AWAY
        }

    def f_sends(src, dst, send, recv):
        return [out_copy(src, dst, send, recv, rel, 0, 0) for rel in FAR if rel]

    narrow = f1_src.at[:, :, :PORT], f1_rcv.at[:, :, :PORT]

    base_out = term_sends(base_src, base_rcv, base_send, base_recv, 0)
    own_out = term_sends(own_src, fwd_rcv, own_send, fwd_recv, 0)
    f0_out = f_sends(*narrow, f1_send, f1_recv)

    def ring(dz, sign):
        there = lax.rem(z + SIDE + sign * dz, SIDE)
        slot = z if sign > 0 else there
        return pltpu.make_async_remote_copy(
            q_rcv.at[slot], q_rcv.at[slot], q_send.at[dz], q_recv.at[dz],
            device_id={"leaf": x * SIDE + there}, device_id_type=MESH,
        )

    fwd_out = term_sends(fwd_src, fwd_rcv, fwd_send, fwd_recv, 1)
    bwd_out = term_sends(bwd_src, bwd_rcv, bwd_send, bwd_recv, -1)
    f1_out = f_sends(f1_src, f1_rcv, f1_send, f1_recv)
    f2_out = f_sends(f2_src, f2_rcv, f2_send, f2_recv)

    def flat(sends):
        return [copy for dz in AWAY for copy in sends[dz]]

    def neighbour(src, dst, send, recv, step):
        return pltpu.make_async_remote_copy(
            src, dst, send, recv, device_id={"sweep": p + step}, device_id_type=MESH
        )

    aaf_out = neighbour(aaf, aaf_nb, aa_send.at[0], aa_recv.at[0], -1)
    aab_out = neighbour(aab, aab_nb, aa_send.at[1], aa_recv.at[1], 1)
    uf_out = neighbour(uf_src, uf_rcv, u_send.at[0], u_recv.at[0], 1)
    ub_out = neighbour(ub_src, ub_rcv, u_send.at[1], u_recv.at[1], -1)

    for copy in late:
        copy.start()

    @pl.when(p == 0)
    def _():
        whole.start()

    for copy in flat(base_out):
        copy.start()
    base_rcv[k] = base_src[z]

    def product(left_re, left_im, right, out):
        @pl.loop(0, SEP // WIDE)
        def _(i):
            cols = pl.ds(pl.multiple_of(i * WIDE, WIDE), WIDE)
            re, im = right[0, :, cols], right[1, :, cols]
            out[0, :, cols] = (dot(left_re, re) - dot(left_im, im)).astype(BF16)
            out[1, :, cols] = (dot(left_re, im) + dot(left_im, re)).astype(BF16)

    def picked(at):
        return (
            dot(selt[at], lv[0, :, :PORT]).astype(BF16),
            dot(selt[at], lv[1, :, :PORT]).astype(BF16),
        )

    @pl.when(p > 0)
    def _():
        left = picked(0)
        product(left[0], left[1], av, aaf)

    @pl.when((p > 0) & (p != CALLER + 1))
    def _():
        aaf_out.start()

    def give_back():
        left = picked(1)
        product(left[0], left[1], av, aab)
        aab_out.start()

    @pl.when((p > CALLER) & (p < last))
    def _():
        give_back()

    for at in range(2):
        for part in range(2):
            lq[at, part] = dot(lv[part, :PORT, :], sel[at]).astype(BF16)

    def resplit():
        @pl.when(first)
        def _():
            pl.semaphore_wait(go_sem, 1)
            for dz in (2,):
                piece(dz).start()

        @pl.when(jnp.logical_not(first))
        def _():
            pl.semaphore_wait(turn_sem, 1)
            for dz in range(1, SIDE):
                piece(dz).start()

        late[1].wait()
        for dz in range(1, SIDE):
            piece_in(dz).wait_recv()

        @pl.when(first)
        def _():
            pl.semaphore_signal(turn_sem, inc=1, device_id={"sweep": p - 1}, device_id_type=MESH)

        for part in range(2):
            f2d[part] = f2t[part].T

    @pl.when(p > 0)
    def _():
        resplit()

    late[0].wait()

    def summed(src, dst, send, recv, step, total):
        for rel in NEAR:
            if step or rel:
                in_copy(src, dst, send, recv, rel, step).wait_recv()
            total = total + dst[origin(rel)].astype(F32)
        return total

    def ask(total, src, dst, out):
        part = cmul(-total, f2d[0], f2d[1]).astype(BF16)
        src[0] = part
        for copy in out:
            copy.start()
        dst[k] = part

    def answer(src, dst, send, recv, old, pieces):
        corr = jnp.zeros((2 * SRC, PORT), F32)
        for dx in reversed(AWAY):
            blk = lax.rem(x + SIDE - dx, SIDE)
            for dz in reversed(AWAY):
                if dx or dz:
                    in_copy(src, dst, send, recv, dx * SIDE + dz, 0).wait_recv()
            parts = [dst[blk * SIDE + row].astype(F32) for row in range(SIDE)]
            if pieces:
                total = jnp.concatenate([part[:, :OWN] for part in parts], axis=1)
            else:
                total = (parts[0] + parts[1]) + (parts[2] + parts[3])
            rows = block_of(blk)
            corr = corr + cmul(total, cv[0, rows, :], cv[1, rows, :])
            f1_s[blk] = f1_s[blk] + total if old else total
        corr_s[...] = corr

    def shifted(blk, plane):
        lane = lax.rem(lax.broadcasted_iota(jnp.int32, blk.shape, 1), PLANES)
        only = jnp.where(lane == plane, blk, 0.0)
        return pltpu.roll(only, (BLK - PLANES + 1) if plane else (PLANES - 1), axis=1)

    def pass_on(na, src, out, plane):
        corr = corr_s[...]
        corr_re, corr_im = corr.astype(BF16), turned(corr).astype(BF16)
        for dz in AWAY:
            at = lax.rem(z + dz, SIDE)
            cols = block_of(at)
            term = pre_s[at] - (dot(corr_re, na[0, :, cols]) + dot(corr_im, na[1, :, cols]))
            src[at] = term.astype(BF16)
            if dz == 0:
                src[SIDE] = (term - shifted(f1_s[at], plane)).astype(BF16)
            for copy in out[dz]:
                copy.start()

    def edge(at, plane, src, copy):
        src[:, :PORT] = (is_s[...] - cmul(corr_s[...], lq[at, 0], lq[at, 1])).astype(BF16)
        src[:, PORT:] = shifted(f1_s[z], plane).astype(BF16)
        copy.start()

    def prepare(at, inner, aa):
        is_s[...] = dot(inner.astype(BF16), sel[at])
        for blk in range(SIDE):
            cols = slice(blk * BLK, (blk + 1) * BLK)
            pre_s[blk] = cmul(is_s[...], aa[0, :, cols], aa[1, :, cols])

    def corrected(inner):
        return (inner - cmul(corr_s[...], lv[0, :PORT, :], lv[1, :PORT, :])) * live

    zero = jnp.zeros((2 * SRC, BLK), F32)

    def take_edge():
        neighbour(uf_src, uf_rcv, u_send.at[0], u_recv.at[0], -1).wait_recv()

    def take_inner():
        spread = dot(uf_rcv[:, :PORT], selt[0])
        inner_s[...] = inner_s[...] + cmul(spread, lv[0], lv[1])

    @pl.when(p == 0)
    def _():
        total = summed(base_src, base_rcv, base_send, base_recv, 0, zero)
        let_go()
        q_rcv[z] = (-total).astype(BF16)
        for dz in AWAY[:-1]:
            ring(dz, 1).start()
        for dz in AWAY[:-1]:
            ring(dz, -1).wait_recv()
        whole.wait()
        full = jnp.concatenate([q_rcv[at].astype(F32) for at in range(SIDE)], axis=1)
        part = dot_t(full.astype(BF16), fo[0]) + dot_t(turned(full).astype(BF16), fo[1])
        f1_src[0, :, :OWN] = part.astype(BF16)
        for copy in f0_out:
            copy.start()
        f1_rcv[k, :, :OWN] = part.astype(BF16)

    @pl.when((p > 0) & (p != CALLER + 1))
    def _():
        total = summed(base_src, base_rcv, base_send, base_recv, 0, zero)
        total = summed(fwd_src, fwd_rcv, fwd_send, fwd_recv, 1, total)
        ask(total, f1_src, f1_rcv, f1_out)
        take_edge()
        take_inner()

    @pl.when(p == CALLER + 1)
    def _():
        total = summed(base_src, base_rcv, base_send, base_recv, 0, zero)
        take_edge()
        for dz in AWAY:
            at = lax.rem(z + dz, SIDE)
            cols = block_of(at)
            term = cmul(uf_rcv[:, :PORT].astype(F32), aaf[0, :, cols], aaf[1, :, cols])
            own_src[at] = term.astype(BF16)
            for copy in own_out[dz]:
                copy.start()
        fwd_rcv[k] = (own_src[z].astype(F32) - uf_rcv[:, PORT:].astype(F32)).astype(BF16)
        total = summed(own_src, fwd_rcv, own_send, fwd_recv, 0, total)
        ask(total, f1_src, f1_rcv, f1_out)
        take_inner()

    @pl.when(p == CALLER)
    def _():
        is_s[...] = dot(inner_s[...].astype(BF16), sel[1])

    @pl.when((p < last) & (p != CALLER))
    def _():
        neighbour(aaf, aaf_nb, aa_send.at[0], aa_recv.at[0], 1).wait_recv()
        product(lq[1, 0], lq[1, 1], aaf_nb, naf)
        prepare(1, inner_s[...], aaf_nb)

    def take_back():
        neighbour(aab, aab_nb, aa_send.at[1], aa_recv.at[1], -1).wait_recv()
        product(lq[0, 0], lq[0, 1], aab_nb, nab)

    @pl.when(p == last)
    def _():
        take_back()
        prepare(0, inner_s[...], aab_nb)

    @pl.when(p == 0)
    def _():
        answer(*narrow, f1_send, f1_recv, False, True)

    @pl.when(p > 0)
    def _():
        answer(f1_src, f1_rcv, f1_send, f1_recv, False, False)


    @pl.when((p < last) & (p != CALLER))
    def _():
        pass_on(naf, fwd_src, fwd_out, PLANES - 1)

    @pl.when(p < last)
    def _():
        edge(1, PLANES - 1, uf_src, uf_out)

    @pl.when(p == last)
    def _():
        pass_on(nab, bwd_src, bwd_out, 0)
        edge(0, 0, ub_src, ub_out)

    w_s[...] = corrected(inner_s[...])

    @pl.when(p == 0)
    def _():
        resplit()

    @pl.when(p <= CALLER)
    def _():
        give_back()

    @pl.when((p > 0) & (p < last))
    def _():
        take_back()

    @pl.when(p < last)
    def _():
        total = summed(bwd_src, bwd_rcv, bwd_send, bwd_recv, -1, zero)
        ask(total, f2_src, f2_rcv, f2_out)
        neighbour(ub_src, ub_rcv, u_send.at[1], u_recv.at[1], 1).wait_recv()
        spread = dot(ub_rcv[:, :PORT], selt[1])
        innerb_s[...] = cmul(spread, lv[0], lv[1])

    @pl.when((p > 0) & (p < last))
    def _():
        prepare(0, w_s[...] + innerb_s[...], aab_nb)

    @pl.when(p < last)
    def _():
        answer(f2_src, f2_rcv, f2_send, f2_recv, True, False)

    @pl.when((p > 0) & (p < last))
    def _():
        pass_on(nab, bwd_src, bwd_out, 0)
        edge(0, 0, ub_src, ub_out)

    @pl.when(p < last)
    def _():
        w_s[...] = w_s[...] + corrected(innerb_s[...])

    oint_ref[0, 0, 0] = w_s[:SRC, :]
    oint_ref[0, 0, 1] = w_s[SRC:, :]
    block = f1_s[x]
    mine = jnp.zeros((2 * SRC, OWN), F32)
    for owner in range(SIDE):
        mine = jnp.where(z == owner, block[:, owner * OWN : (owner + 1) * OWN], mine)
    osep_ref[0, 0] = mine[:SRC]
    osep_ref[0, 1] = mine[SRC:]

    for dz in range(1, SIDE):
        piece(dz).wait_send()

    @pl.when(p == 0)
    def _():
        for copy in flat(base_out) + f0_out:
            copy.wait_send()
        for dz in AWAY[:-1]:
            ring(dz, 1).wait_send()

    @pl.when(p > 0)
    def _():
        for copy in flat(base_out) + f1_out + flat(bwd_out):
            copy.wait_send()
        ub_out.wait_send()

    @pl.when((p > 0) & (p != CALLER + 1))
    def _():
        aaf_out.wait_send()

    @pl.when(p == CALLER + 1)
    def _():
        for copy in flat(own_out):
            copy.wait_send()

    @pl.when(p < last)
    def _():
        aab_out.wait_send()
        uf_out.wait_send()
        for copy in f2_out:
            copy.wait_send()

    @pl.when((p < last) & (p != CALLER))
    def _():
        for copy in flat(fwd_out):
            copy.wait_send()


def body(rhs_int, rhs_sep, leaf_inv, to_front, to_leaf, front_inv, sizes):
    vmem, hbm = pl.BlockSpec(memory_space=pltpu.VMEM), pl.BlockSpec(memory_space=pltpu.HBM)
    rows = 2 * SRC

    def messages(count, width):
        return pltpu.VMEM((count, rows, width), BF16)

    scratch = [
        pltpu.VMEM((2, SRC, LEAF), F32),
        pltpu.VMEM((2, SRC, OWN), F32),
        pltpu.VMEM((2, LEAF, LEAF), BF16),
        pltpu.VMEM((2, PORT, SEP), BF16),
        pltpu.VMEM((2, SEP, PORT), BF16),
        pltpu.VMEM((2, OWN, SEP), BF16),
        pltpu.VMEM((2, BLK, BLK), BF16),
        pltpu.VMEM((2, BLK, BLK), BF16),
        pltpu.VMEM((SIDE, OWN, BLK), BF16),
        pltpu.VMEM((2, LEAF, PORT), BF16),
        pltpu.VMEM((2, PORT, LEAF), BF16),
    ]
    scratch += [pltpu.VMEM((2, PORT, SEP), BF16)] * 6
    scratch += [
        pltpu.VMEM((2, 2, PORT, PORT), BF16),
        pltpu.VMEM((rows, LEAF), F32),
        pltpu.VMEM((rows, LEAF), F32),
        pltpu.VMEM((rows, LEAF), F32),
        pltpu.VMEM((rows, PORT), F32),
        pltpu.VMEM((SIDE, rows, BLK), F32),
        pltpu.VMEM((SIDE, rows, BLK), F32),
        pltpu.VMEM((rows, PORT), F32),
    ]
    scratch += [messages(SIDE + 1, BLK)] * 4 + [messages(1, BLK)] * 2
    scratch += [pltpu.VMEM((rows, PORT + BLK), BF16)] * 2
    scratch += [messages(SIDE, BLK)] + [messages(GROUP, BLK)] * 5 + [pltpu.VMEM((rows, PORT + BLK), BF16)] * 2
    dma = pltpu.SemaphoreType.DMA
    scratch += [pltpu.SemaphoreType.REGULAR] * 2 + [dma((7,))] + [dma((SIDE,))] * 4 + [dma((2,))] * 4 + [dma((GROUP,))] * 11
    return pl.pallas_call(
        kernel,
        out_shape=(
            jax.ShapeDtypeStruct(rhs_int.shape, F32),
            jax.ShapeDtypeStruct(rhs_sep.shape, F32),
        ),
        in_specs=[hbm, hbm, pl.BlockSpec(memory_space=pltpu.SMEM)] + [hbm] * 4,
        out_specs=(vmem, vmem),
        scratch_shapes=scratch,
        compiler_params=pltpu.CompilerParams(
            collective_id=0, has_side_effects=True, vmem_limit_bytes=53 << 20
        ),
    )(rhs_int, rhs_sep, sizes, leaf_inv, to_front, to_leaf, front_inv.swapaxes(2, 3))


def solution(mesh):
    placed = (
        P("sweep", "leaf", None, None, None),
        P("sweep", None, None, "leaf"),
        P("sweep", "leaf", None, None, None),
        P("sweep", "leaf", None, None, None),
        P("sweep", "leaf", None, None, None),
        P("sweep", None, None, "leaf"),
        P("sweep", "leaf"),
    )
    return jax.shard_map(
        body,
        mesh=mesh,
        in_specs=placed,
        out_specs=(P("sweep", "leaf", None, None, None), P("sweep", None, None, "leaf")),
        check_vma=False,
    )
```

```python
import functools

import jax
import jax.numpy as jnp
from jax import lax
from jax.experimental import pallas as pl
from jax.experimental.pallas import tpu as pltpu
from jax.sharding import PartitionSpec as P

MESH = pl.DeviceIdType.MESH
F32, BF16 = jnp.float32, jnp.bfloat16
PORT = 256
PLANES = 4
SIDE = 4
GROUP = SIDE * SIDE
LEAF = 1024
SEP = 2560
OWN = SEP // GROUP
BLK = SEP // SIDE
SRC = 4
CALLER = 1
WIDE = 512


def hops(rel):
    return sum(min(d, SIDE - d) for d in divmod(rel, SIDE))


NEAR = sorted(range(GROUP), key=hops)
FAR = sorted(range(GROUP), key=lambda rel: -hops(rel))
AWAY = (2, 1, 3, 0)


def dot(lhs, rhs):
    return jnp.dot(lhs, rhs, preferred_element_type=F32)


def dot_t(lhs, rhs):
    return lax.dot_general(lhs, rhs, (((1,), (1,)), ((), ())), preferred_element_type=F32)


def turned(vec):
    row = lax.broadcasted_iota(jnp.int32, vec.shape, 0)
    return jnp.where(row < SRC, -1.0, 1.0) * pltpu.roll(vec, SRC, axis=0)


def cmul(vec, w_re, w_im):
    return dot(vec.astype(BF16), w_re) + dot(turned(vec).astype(BF16), w_im)


def kernel(
    rint_hbm, rsep_hbm, fs_ref, l_hbm, a_hbm, c_hbm, f_hbm,
    oint_ref, osep_ref,
    rint_ref, rsep_ref, lv, av, cv, fo, f2t, f2d, place, sel, selt, aaf, aab, naf, nab, aaf_nb, aab_nb, lq,
    inner_s, innerb_s, w_s, corr_s, f1_s, pre_s, is_s,
    base_src, fwd_src, bwd_src, own_src, f1_src, f2_src, uf_src, ub_src, q_rcv,
    base_rcv, fwd_rcv, bwd_rcv, f1_rcv, f2_rcv, uf_rcv, ub_rcv,
    go_sem, turn_sem, load_sem, q_send, q_recv, fp_send, fp_recv, aa_send, aa_recv, u_send, u_recv,
    base_send, base_recv, fwd_send, fwd_recv, bwd_send, bwd_recv,
    own_send, f1_send, f1_recv, f2_send, f2_recv,
):
    p, k = lax.axis_index("sweep"), lax.axis_index("leaf")
    last = lax.axis_size("sweep") - 1
    x, z = k // SIDE, lax.rem(k, SIDE)

    def to(rel):
        dx, dz = divmod(rel, SIDE)
        return lax.rem(x + dx, SIDE) * SIDE + lax.rem(z + dz, SIDE)

    def origin(rel):
        dx, dz = divmod(rel, SIDE)
        return lax.rem(x + SIDE - dx, SIDE) * SIDE + lax.rem(z + SIDE - dz, SIDE)

    def block_of(side):
        return pl.ds(pl.multiple_of(side * BLK, BLK), BLK)

    def owned_by(side):
        return pl.ds(pl.multiple_of(side * OWN, OWN), OWN)

    early = [
        pltpu.make_async_copy(rint_hbm.at[0, 0], rint_ref, load_sem.at[0]),
        pltpu.make_async_copy(l_hbm.at[0, 0], lv, load_sem.at[1]),
        pltpu.make_async_copy(rsep_hbm.at[0], rsep_ref, load_sem.at[2]),
        pltpu.make_async_copy(a_hbm.at[0, 0], av, load_sem.at[3]),
    ]
    late = [
        pltpu.make_async_copy(c_hbm.at[0, 0], cv, load_sem.at[4]),
        pltpu.make_async_copy(
            f_hbm.at[0, :, :, block_of(z)], f2t.at[:, owned_by(z), :], load_sem.at[5]
        ),
    ]
    whole = pltpu.make_async_copy(f_hbm.at[0], fo, load_sem.at[6])
    for load in early:
        load.start()

    barrier = pltpu.get_barrier_semaphore()
    for rel in range(1, GROUP):
        pl.semaphore_signal(barrier, inc=1, device_id={"leaf": to(rel)}, device_id_type=MESH)

    @pl.when(p < last)
    def _():
        for leaf in range(GROUP):
            pl.semaphore_signal(
                barrier, inc=1, device_id={"sweep": p + 1, "leaf": leaf}, device_id_type=MESH
            )

    @pl.when(p > 0)
    def _():
        for leaf in range(GROUP):
            pl.semaphore_signal(
                barrier, inc=1, device_id={"sweep": p - 1, "leaf": leaf}, device_id_type=MESH
            )

    size = fs_ref[0, 0] + PORT
    for at, plane in ((0, 0), (1, PLANES - 1)):
        cell = lax.broadcasted_iota(jnp.int32, (LEAF, PORT), 0)
        hit = (cell == lax.broadcasted_iota(jnp.int32, (LEAF, PORT), 1) * PLANES + plane) & (cell < size)
        sel[at] = jnp.where(hit, 1.0, 0.0).astype(BF16)
        cell = lax.broadcasted_iota(jnp.int32, (PORT, LEAF), 1)
        hit = (cell == lax.broadcasted_iota(jnp.int32, (PORT, LEAF), 0) * PLANES + plane) & (cell < size)
        selt[at] = jnp.where(hit, 1.0, 0.0).astype(BF16)

    for blk in range(SIDE):
        hit = (
            lax.broadcasted_iota(jnp.int32, (OWN, BLK), 1) + blk * BLK
            == lax.broadcasted_iota(jnp.int32, (OWN, BLK), 0) + k * OWN
        )
        place[blk] = jnp.where(hit, 1.0, 0.0).astype(BF16)

    col = lax.broadcasted_iota(jnp.int32, (1, LEAF), 1)
    live = jnp.where(col < size, 1.0, 0.0).astype(F32)

    def rows_of(ref):
        return jnp.concatenate([ref[0], ref[1]], axis=0)

    early[0].wait()
    early[1].wait()
    inner_s[...] = cmul(rows_of(rint_ref) * live, lv[0], lv[1])
    early[2].wait()
    early[3].wait()
    own = rows_of(rsep_ref).astype(BF16)
    for blk in range(SIDE):
        cols = slice(blk * BLK, (blk + 1) * BLK)
        term = cmul(inner_s[:, :PORT], av[0, :, cols], av[1, :, cols]) - dot(own, place[blk])
        base_src[blk] = term.astype(BF16)

    @pl.when((p > 0) & (p < last))
    def _():
        pl.semaphore_wait(barrier, 3 * GROUP - 1)

    @pl.when((p == 0) | (p == last))
    def _():
        pl.semaphore_wait(barrier, 2 * GROUP - 1)

    def piece(dz):
        there = lax.rem(z + dz, SIDE)
        return pltpu.make_async_remote_copy(
            f_hbm.at[0, :, :, block_of(there)],
            f2t.at[:, owned_by(z), :],
            fp_send.at[dz],
            fp_recv.at[dz],
            device_id={"leaf": x * SIDE + there},
            device_id_type=MESH,
        )

    def piece_in(dz):
        here = lax.rem(z + SIDE - dz, SIDE)
        return pltpu.make_async_remote_copy(
            f_hbm.at[0, :, :, block_of(z)],
            f2t.at[:, owned_by(here), :],
            fp_send.at[dz],
            fp_recv.at[dz],
            device_id={"leaf": x * SIDE + here},
            device_id_type=MESH,
        )

    first = lax.rem(p, 2) == 1

    @pl.when(first)
    def _():
        for dz in (1, SIDE - 1):
            piece(dz).start()

    def let_go():
        pl.semaphore_signal(go_sem, inc=1, device_id={"sweep": p + 1}, device_id_type=MESH)

    @pl.when(jnp.logical_not(first) & (p > 0))
    def _():
        let_go()

    def out_copy(src, dst, send, recv, rel, slot, step):
        there = {"leaf": to(rel)}
        if step:
            there["sweep"] = p + step
        return pltpu.make_async_remote_copy(
            src.at[slot], dst.at[k], send.at[rel], recv.at[rel], device_id=there, device_id_type=MESH
        )

    def in_copy(src, dst, send, recv, rel, step):
        there = {"leaf": origin(rel)}
        if step:
            there["sweep"] = p - step
        return pltpu.make_async_remote_copy(
            src.at[0], dst.at[origin(rel)], send.at[rel], recv.at[rel],
            device_id=there, device_id_type=MESH,
        )

    def term_sends(src, dst, send, recv, step):
        return {
            dz: [
                out_copy(
                    src, dst, send, recv, dx * SIDE + dz,
                    SIDE if dx == dz == 0 else lax.rem(z + dz, SIDE), step,
                )
                for dx in AWAY
                if step or dx or dz
            ]
            for dz in AWAY
        }

    def f_sends(src, dst, send, recv):
        return [out_copy(src, dst, send, recv, rel, 0, 0) for rel in FAR if rel]

    narrow = f1_src.at[:, :, :PORT], f1_rcv.at[:, :, :PORT]

    base_out = term_sends(base_src, base_rcv, base_send, base_recv, 0)
    own_out = term_sends(own_src, fwd_rcv, own_send, fwd_recv, 0)
    f0_out = f_sends(*narrow, f1_send, f1_recv)

    def ring(dz, sign):
        there = lax.rem(z + SIDE + sign * dz, SIDE)
        slot = z if sign > 0 else there
        return pltpu.make_async_remote_copy(
            q_rcv.at[slot], q_rcv.at[slot], q_send.at[dz], q_recv.at[dz],
            device_id={"leaf": x * SIDE + there}, device_id_type=MESH,
        )

    fwd_out = term_sends(fwd_src, fwd_rcv, fwd_send, fwd_recv, 1)
    bwd_out = term_sends(bwd_src, bwd_rcv, bwd_send, bwd_recv, -1)
    f1_out = f_sends(f1_src, f1_rcv, f1_send, f1_recv)
    f2_out = f_sends(f2_src, f2_rcv, f2_send, f2_recv)

    def flat(sends):
        return [copy for dz in AWAY for copy in sends[dz]]

    def neighbour(src, dst, send, recv, step):
        return pltpu.make_async_remote_copy(
            src, dst, send, recv, device_id={"sweep": p + step}, device_id_type=MESH
        )

    aaf_out = neighbour(aaf, aaf_nb, aa_send.at[0], aa_recv.at[0], -1)
    aab_out = neighbour(aab, aab_nb, aa_send.at[1], aa_recv.at[1], 1)
    uf_out = neighbour(uf_src, uf_rcv, u_send.at[0], u_recv.at[0], 1)
    ub_out = neighbour(ub_src, ub_rcv, u_send.at[1], u_recv.at[1], -1)

    for copy in late:
        copy.start()

    @pl.when(p == 0)
    def _():
        whole.start()

    for copy in flat(base_out):
        copy.start()
    base_rcv[k] = base_src[z]

    def product(left_re, left_im, right, out):
        @pl.loop(0, SEP // WIDE)
        def _(i):
            cols = pl.ds(pl.multiple_of(i * WIDE, WIDE), WIDE)
            re, im = right[0, :, cols], right[1, :, cols]
            out[0, :, cols] = (dot(left_re, re) - dot(left_im, im)).astype(BF16)
            out[1, :, cols] = (dot(left_re, im) + dot(left_im, re)).astype(BF16)

    def picked(at):
        return (
            dot(selt[at], lv[0, :, :PORT]).astype(BF16),
            dot(selt[at], lv[1, :, :PORT]).astype(BF16),
        )

    @pl.when(p > 0)
    def _():
        left = picked(0)
        product(left[0], left[1], av, aaf)

    @pl.when((p > 0) & (p != CALLER + 1))
    def _():
        aaf_out.start()

    def give_back():
        left = picked(1)
        product(left[0], left[1], av, aab)
        aab_out.start()

    @pl.when((p > CALLER) & (p < last))
    def _():
        give_back()

    for at in range(2):
        for part in range(2):
            lq[at, part] = dot(lv[part, :PORT, :], sel[at]).astype(BF16)

    def resplit():
        @pl.when(first)
        def _():
            pl.semaphore_wait(go_sem, 1)
            for dz in (2,):
                piece(dz).start()

        @pl.when(jnp.logical_not(first))
        def _():
            pl.semaphore_wait(turn_sem, 1)
            for dz in range(1, SIDE):
                piece(dz).start()

        late[1].wait()
        for dz in range(1, SIDE):
            piece_in(dz).wait_recv()

        @pl.when(first & (p != CALLER))
        def _():
            pl.semaphore_signal(turn_sem, inc=1, device_id={"sweep": p - 1}, device_id_type=MESH)

        for part in range(2):
            f2d[part] = f2t[part].T

    @pl.when(p > 0)
    def _():
        resplit()

    late[0].wait()

    def summed(src, dst, send, recv, step, total):
        for rel in NEAR:
            if step or rel:
                in_copy(src, dst, send, recv, rel, step).wait_recv()
            total = total + dst[origin(rel)].astype(F32)
        return total

    def ask(total, src, dst, out):
        part = cmul(-total, f2d[0], f2d[1]).astype(BF16)
        src[0] = part
        for copy in out:
            copy.start()
        dst[k] = part

    def answer(src, dst, send, recv, old, pieces):
        corr = jnp.zeros((2 * SRC, PORT), F32)
        for dx in reversed(AWAY):
            blk = lax.rem(x + SIDE - dx, SIDE)
            for dz in reversed(AWAY):
                if dx or dz:
                    in_copy(src, dst, send, recv, dx * SIDE + dz, 0).wait_recv()
            parts = [dst[blk * SIDE + row].astype(F32) for row in range(SIDE)]
            if pieces:
                total = jnp.concatenate([part[:, :OWN] for part in parts], axis=1)
            else:
                total = (parts[0] + parts[1]) + (parts[2] + parts[3])
            rows = block_of(blk)
            corr = corr + cmul(total, cv[0, rows, :], cv[1, rows, :])
            f1_s[blk] = f1_s[blk] + total if old else total
        corr_s[...] = corr

    def shifted(blk, plane):
        lane = lax.rem(lax.broadcasted_iota(jnp.int32, blk.shape, 1), PLANES)
        only = jnp.where(lane == plane, blk, 0.0)
        return pltpu.roll(only, (BLK - PLANES + 1) if plane else (PLANES - 1), axis=1)

    def pass_on(na, src, out, plane):
        corr = corr_s[...]
        corr_re, corr_im = corr.astype(BF16), turned(corr).astype(BF16)
        for dz in AWAY:
            at = lax.rem(z + dz, SIDE)
            cols = block_of(at)
            term = pre_s[at] - (dot(corr_re, na[0, :, cols]) + dot(corr_im, na[1, :, cols]))
            src[at] = term.astype(BF16)
            if dz == 0:
                src[SIDE] = (term - shifted(f1_s[at], plane)).astype(BF16)
            for copy in out[dz]:
                copy.start()

    def edge(at, plane, src, copy):
        src[:, :PORT] = (is_s[...] - cmul(corr_s[...], lq[at, 0], lq[at, 1])).astype(BF16)
        src[:, PORT:] = shifted(f1_s[z], plane).astype(BF16)
        copy.start()

    def prepare(at, inner, aa):
        is_s[...] = dot(inner.astype(BF16), sel[at])
        for blk in range(SIDE):
            cols = slice(blk * BLK, (blk + 1) * BLK)
            pre_s[blk] = cmul(is_s[...], aa[0, :, cols], aa[1, :, cols])

    def corrected(inner):
        return (inner - cmul(corr_s[...], lv[0, :PORT, :], lv[1, :PORT, :])) * live

    zero = jnp.zeros((2 * SRC, BLK), F32)

    def take_edge():
        neighbour(uf_src, uf_rcv, u_send.at[0], u_recv.at[0], -1).wait_recv()

    def take_inner():
        spread = dot(uf_rcv[:, :PORT], selt[0])
        inner_s[...] = inner_s[...] + cmul(spread, lv[0], lv[1])

    @pl.when(p == 0)
    def _():
        total = summed(base_src, base_rcv, base_send, base_recv, 0, zero)
        let_go()
        q_rcv[z] = (-total).astype(BF16)
        for dz in AWAY[:-1]:
            ring(dz, 1).start()
        for dz in AWAY[:-1]:
            ring(dz, -1).wait_recv()
        whole.wait()
        full = jnp.concatenate([q_rcv[at].astype(F32) for at in range(SIDE)], axis=1)
        part = dot_t(full.astype(BF16), fo[0]) + dot_t(turned(full).astype(BF16), fo[1])
        f1_src[0, :, :OWN] = part.astype(BF16)
        for copy in f0_out:
            copy.start()
        f1_rcv[k, :, :OWN] = part.astype(BF16)

    @pl.when((p > 0) & (p != CALLER + 1))
    def _():
        total = summed(base_src, base_rcv, base_send, base_recv, 0, zero)
        total = summed(fwd_src, fwd_rcv, fwd_send, fwd_recv, 1, total)
        ask(total, f1_src, f1_rcv, f1_out)
        take_edge()
        take_inner()

    @pl.when(p == CALLER + 1)
    def _():
        total = summed(base_src, base_rcv, base_send, base_recv, 0, zero)
        take_edge()
        for dz in AWAY:
            at = lax.rem(z + dz, SIDE)
            cols = block_of(at)
            term = cmul(uf_rcv[:, :PORT].astype(F32), aaf[0, :, cols], aaf[1, :, cols])
            own_src[at] = term.astype(BF16)
            for copy in own_out[dz]:
                copy.start()
        fwd_rcv[k] = (own_src[z].astype(F32) - uf_rcv[:, PORT:].astype(F32)).astype(BF16)
        total = summed(own_src, fwd_rcv, own_send, fwd_recv, 0, total)
        ask(total, f1_src, f1_rcv, f1_out)
        take_inner()

    @pl.when(p == CALLER)
    def _():
        is_s[...] = dot(inner_s[...].astype(BF16), sel[1])

    @pl.when((p < last) & (p != CALLER))
    def _():
        neighbour(aaf, aaf_nb, aa_send.at[0], aa_recv.at[0], 1).wait_recv()
        product(lq[1, 0], lq[1, 1], aaf_nb, naf)
        prepare(1, inner_s[...], aaf_nb)

    def take_back():
        neighbour(aab, aab_nb, aa_send.at[1], aa_recv.at[1], -1).wait_recv()
        product(lq[0, 0], lq[0, 1], aab_nb, nab)

    @pl.when(p == last)
    def _():
        take_back()
        prepare(0, inner_s[...], aab_nb)

    @pl.when(p == 0)
    def _():
        answer(*narrow, f1_send, f1_recv, False, True)

    @pl.when(p > 0)
    def _():
        answer(f1_src, f1_rcv, f1_send, f1_recv, False, False)


    @pl.when((p < last) & (p != CALLER))
    def _():
        pass_on(naf, fwd_src, fwd_out, PLANES - 1)

    @pl.when(p < last)
    def _():
        edge(1, PLANES - 1, uf_src, uf_out)

    @pl.when(p == last)
    def _():
        pass_on(nab, bwd_src, bwd_out, 0)
        edge(0, 0, ub_src, ub_out)

    @pl.when(p == CALLER)
    def _():
        pl.semaphore_signal(turn_sem, inc=1, device_id={"sweep": p - 1}, device_id_type=MESH)

    w_s[...] = corrected(inner_s[...])

    @pl.when(p == 0)
    def _():
        resplit()

    @pl.when(p <= CALLER)
    def _():
        give_back()

    @pl.when((p > 0) & (p < last))
    def _():
        take_back()

    @pl.when(p < last)
    def _():
        total = summed(bwd_src, bwd_rcv, bwd_send, bwd_recv, -1, zero)
        ask(total, f2_src, f2_rcv, f2_out)
        neighbour(ub_src, ub_rcv, u_send.at[1], u_recv.at[1], 1).wait_recv()
        spread = dot(ub_rcv[:, :PORT], selt[1])
        innerb_s[...] = cmul(spread, lv[0], lv[1])

    @pl.when((p > 0) & (p < last))
    def _():
        prepare(0, w_s[...] + innerb_s[...], aab_nb)

    @pl.when(p < last)
    def _():
        answer(f2_src, f2_rcv, f2_send, f2_recv, True, False)

    @pl.when((p > 0) & (p < last))
    def _():
        pass_on(nab, bwd_src, bwd_out, 0)
        edge(0, 0, ub_src, ub_out)

    @pl.when(p < last)
    def _():
        w_s[...] = w_s[...] + corrected(innerb_s[...])

    oint_ref[0, 0, 0] = w_s[:SRC, :]
    oint_ref[0, 0, 1] = w_s[SRC:, :]
    block = f1_s[x]
    mine = jnp.zeros((2 * SRC, OWN), F32)
    for owner in range(SIDE):
        mine = jnp.where(z == owner, block[:, owner * OWN : (owner + 1) * OWN], mine)
    osep_ref[0, 0] = mine[:SRC]
    osep_ref[0, 1] = mine[SRC:]

    for dz in range(1, SIDE):
        piece(dz).wait_send()

    @pl.when(p == 0)
    def _():
        for copy in flat(base_out) + f0_out:
            copy.wait_send()
        for dz in AWAY[:-1]:
            ring(dz, 1).wait_send()

    @pl.when(p > 0)
    def _():
        for copy in flat(base_out) + f1_out + flat(bwd_out):
            copy.wait_send()
        ub_out.wait_send()

    @pl.when((p > 0) & (p != CALLER + 1))
    def _():
        aaf_out.wait_send()

    @pl.when(p == CALLER + 1)
    def _():
        for copy in flat(own_out):
            copy.wait_send()

    @pl.when(p < last)
    def _():
        aab_out.wait_send()
        uf_out.wait_send()
        for copy in f2_out:
            copy.wait_send()

    @pl.when((p < last) & (p != CALLER))
    def _():
        for copy in flat(fwd_out):
            copy.wait_send()


def body(rhs_int, rhs_sep, leaf_inv, to_front, to_leaf, front_inv, sizes):
    vmem, hbm = pl.BlockSpec(memory_space=pltpu.VMEM), pl.BlockSpec(memory_space=pltpu.HBM)
    rows = 2 * SRC

    def messages(count, width):
        return pltpu.VMEM((count, rows, width), BF16)

    scratch = [
        pltpu.VMEM((2, SRC, LEAF), F32),
        pltpu.VMEM((2, SRC, OWN), F32),
        pltpu.VMEM((2, LEAF, LEAF), BF16),
        pltpu.VMEM((2, PORT, SEP), BF16),
        pltpu.VMEM((2, SEP, PORT), BF16),
        pltpu.VMEM((2, OWN, SEP), BF16),
        pltpu.VMEM((2, BLK, BLK), BF16),
        pltpu.VMEM((2, BLK, BLK), BF16),
        pltpu.VMEM((SIDE, OWN, BLK), BF16),
        pltpu.VMEM((2, LEAF, PORT), BF16),
        pltpu.VMEM((2, PORT, LEAF), BF16),
    ]
    scratch += [pltpu.VMEM((2, PORT, SEP), BF16)] * 6
    scratch += [
        pltpu.VMEM((2, 2, PORT, PORT), BF16),
        pltpu.VMEM((rows, LEAF), F32),
        pltpu.VMEM((rows, LEAF), F32),
        pltpu.VMEM((rows, LEAF), F32),
        pltpu.VMEM((rows, PORT), F32),
        pltpu.VMEM((SIDE, rows, BLK), F32),
        pltpu.VMEM((SIDE, rows, BLK), F32),
        pltpu.VMEM((rows, PORT), F32),
    ]
    scratch += [messages(SIDE + 1, BLK)] * 4 + [messages(1, BLK)] * 2
    scratch += [pltpu.VMEM((rows, PORT + BLK), BF16)] * 2
    scratch += [messages(SIDE, BLK)] + [messages(GROUP, BLK)] * 5 + [pltpu.VMEM((rows, PORT + BLK), BF16)] * 2
    dma = pltpu.SemaphoreType.DMA
    scratch += [pltpu.SemaphoreType.REGULAR] * 2 + [dma((7,))] + [dma((SIDE,))] * 4 + [dma((2,))] * 4 + [dma((GROUP,))] * 11
    return pl.pallas_call(
        kernel,
        out_shape=(
            jax.ShapeDtypeStruct(rhs_int.shape, F32),
            jax.ShapeDtypeStruct(rhs_sep.shape, F32),
        ),
        in_specs=[hbm, hbm, pl.BlockSpec(memory_space=pltpu.SMEM)] + [hbm] * 4,
        out_specs=(vmem, vmem),
        scratch_shapes=scratch,
        compiler_params=pltpu.CompilerParams(
            collective_id=0, has_side_effects=True, vmem_limit_bytes=53 << 20
        ),
    )(rhs_int, rhs_sep, sizes, leaf_inv, to_front, to_leaf, front_inv.swapaxes(2, 3))


def solution(mesh):
    placed = (
        P("sweep", "leaf", None, None, None),
        P("sweep", None, None, "leaf"),
        P("sweep", "leaf", None, None, None),
        P("sweep", "leaf", None, None, None),
        P("sweep", "leaf", None, None, None),
        P("sweep", None, None, "leaf"),
        P("sweep", "leaf"),
    )
    return jax.shard_map(
        body,
        mesh=mesh,
        in_specs=placed,
        out_specs=(P("sweep", "leaf", None, None, None), P("sweep", None, None, "leaf")),
        check_vma=False,
    )
```
